512 devices in a mesh: seq: 64 (over y, z), head: 8 (over x, core).
Axes of the slice: x: 4, y: 8, z: 8, core: 2. Of those that a mesh axis runs over, the one named last changes fastest.
Arguments:
- query_input: bfloat16 [16384, 2048], P('seq', 'head'), may hold values from -6 to 6
- key_input: bfloat16 [16384, 2048], P('seq', 'head'), may hold values from -6 to 6
- value_input: bfloat16 [16384, 4096], P('seq', 'head'), may hold values from -6 to 6
- kernel_taps: float32 [2, 4, 2048], P(None, None, 'head'), may hold values from -3 to 3
- input_gate: float32 [8, 16384], P('head', 'seq'), may hold values from -6 to 300
- forget_gate: float32 [8, 16384], P('head', 'seq'), may hold values from -0.5 to 16
- request_lengths: int32 [4], replicated, may hold values from 1 to 8192, as said below
- output_weight: bfloat16 [4096, 2048], P('head'), may hold values from -0.09375 to 0.09375
Outputs:
- mixed_out: bfloat16 [16384, 2048], P('seq', 'head')
The draws below stay inside these ranges and needn't reach their ends.
Inputs may be any that keep to these rules, and one draw needn't show every extreme that they name: `request_lengths`: the lengths sum to 16384; the longest request has exactly 8192 tokens.
All inputs are finite; a program needn't handle non-finite values.
Results may differ from the reference program's by a relative error of at most 0.012.
Values may be sent and summed in bfloat16 or wider, within the bound.
A program may use at most 128 MiB of HBM per device.

```python
import math
import jax
import jax.numpy as jnp
from jax import lax

HEADS = 8
DQK = 256
DV = 512
OUT_COLS = 2048
KCONV = 4
REQS = 4
TOK_DEV = 256
PACKED_TOKENS = 16384


def request_sizes(key):
    base_key = jax.random.fold_in(key, 7001)
    cut_key, order_key = jax.random.split(base_key)
    remaining = PACKED_TOKENS - PACKED_TOKENS // 2
    cut_points = jnp.sort(jax.random.permutation(cut_key, remaining - 1)[:REQS - 2].astype(jnp.int32) + 1)
    edges = jnp.concatenate([jnp.zeros((1,), jnp.int32), cut_points, jnp.full((1,), remaining, jnp.int32)])
    smaller = edges[1:] - edges[:-1]
    sizes_all = jnp.concatenate([jnp.full((1,), PACKED_TOKENS // 2, jnp.int32), smaller])
    return sizes_all[jax.random.permutation(order_key, REQS)].astype(jnp.int32)


def draw_request_lengths(key, part):
    return request_sizes(key)


def draw_input_gate(key, part):
    gate_key = jax.random.fold_in(key, 7002)
    random_keys = jax.random.split(gate_key, 1)
    return 1.5 * jax.random.truncated_normal(random_keys[0], -4.0, 4.0, (HEADS, PACKED_TOKENS), jnp.float32)


def draw_forget_gate(key, part):
    gate_key = jax.random.fold_in(key, 7003)
    random_keys = jax.random.split(gate_key, 7)
    head_order = jax.random.permutation(random_keys[0], HEADS)
    fast_count = jax.random.randint(random_keys[1], (), 2, HEADS - 1)
    token_factor = jnp.exp(jax.random.uniform(random_keys[2], (HEADS, PACKED_TOKENS), jnp.float32, math.log(0.5), math.log(2.0)))
    quick_heads = (head_order < fast_count)[:, None]
    fast_length = jnp.exp(jax.random.uniform(random_keys[3], (HEADS, 1), jnp.float32, math.log(30.0), math.log(50.0)))
    shard_factor = jnp.exp(jax.random.uniform(random_keys[4], (HEADS, PACKED_TOKENS // TOK_DEV), jnp.float32, math.log(0.5), math.log(2.0)))
    shard_factor = jnp.repeat(shard_factor, TOK_DEV, axis=1)
    gradual_decay_rate = 0.2 / (PACKED_TOKENS // 2) * token_factor * shard_factor
    quick_decay_rate = token_factor / fast_length
    spike_position = jax.random.randint(random_keys[5], (2,), 0, PACKED_TOKENS)
    spike_penalty = jax.random.uniform(random_keys[6], (2,), jnp.float32, 0.2, 0.5)
    spike_count = jnp.arange(PACKED_TOKENS)[None, :] == spike_position[:, None]
    spike_probability = jnp.sum(jnp.where(spike_count, -jnp.log1p(-spike_penalty)[:, None], 0.0), axis=0)
    forget_decay_rate = jnp.where(quick_heads, quick_decay_rate, gradual_decay_rate + spike_probability[None, :])
    return -jnp.log(jnp.expm1(forget_decay_rate))


def block_scale(own_key, extent, cuts, low, largest):
    def one(axis_at, parts):
        heights = jax.random.uniform(jax.random.fold_in(jax.random.fold_in(own_key, 6), axis_at), (parts,), jnp.float32, low / len(cuts), largest / len(cuts))
        return jnp.repeat(jnp.exp(heights), extent[axis_at] // parts).reshape((-1,) + (1,) * (len(extent) - axis_at - 1))

    loudness = one(*cuts[0])
    for cut in cuts[1:]:
        loudness = loudness * one(*cut)
    return loudness


def centred(rng, extent, scale, bound, shards=(), kind=jnp.bfloat16):
    drawn = scale * jax.random.normal(rng, extent, jnp.float32)
    if shards:
        drawn = drawn * block_scale(rng, extent, shards, -0.22, 0.18)
    return jnp.clip(drawn, -bound, bound).astype(kind)


def setup_inputs(seed: int = 0) -> dict:
    splits = jax.random.split(jax.random.key(seed), 9)
    query_input = centred(splits[0], (PACKED_TOKENS, HEADS * DQK), 1.0, 6.0, ((0, 64), (1, 8)))
    key_input = centred(splits[1], (PACKED_TOKENS, HEADS * DQK), 1.0, 6.0, ((0, 64), (1, 8)))
    value_input = centred(splits[2], (PACKED_TOKENS, HEADS * DV), 1.0, 6.0, ((0, 64), (1, 8)))
    kernel_taps = centred(splits[3], (2, KCONV, HEADS * DQK), KCONV ** -0.5, 3.0, ((2, 8),), jnp.float32)
    input_gate = draw_input_gate(jax.random.fold_in(splits[8], 71), 0)
    forget_gate = draw_forget_gate(jax.random.fold_in(splits[8], 71), 0)
    request_lengths = draw_request_lengths(jax.random.fold_in(splits[8], 71), 0)
    output_weight = centred(splits[7], (HEADS * DV, OUT_COLS), (HEADS * DV) ** -0.5, 0.09375, ((0, 8),))
    return {"query_input": query_input, "key_input": key_input, "value_input": value_input, "kernel_taps": kernel_taps, "input_gate": input_gate, "forget_gate": forget_gate, "request_lengths": request_lengths, "output_weight": output_weight}


very_negative = -1e+30

def conv_silu(features, kernel_part, segments):
    length = features.shape[0]
    taps = kernel_part.shape[0]
    padded = jnp.concatenate([jnp.zeros((taps - 1, features.shape[1]), features.dtype), features])
    padded_seg = jnp.concatenate([jnp.full((taps - 1,), -1, jnp.int32), segments])
    running = jnp.zeros(features.shape, jnp.float32)
    for shift_by in range(taps):
        piece_rows = padded[taps - 1 - shift_by:taps - 1 - shift_by + length].astype(jnp.float32)
        same_req = (padded_seg[taps - 1 - shift_by:taps - 1 - shift_by + length] == segments)[:, None]
        running = running + jnp.where(same_req, kernel_part[shift_by][None, :] * piece_rows, 0.0)
    return jax.nn.silu(running).astype(jnp.bfloat16)

def block_pass(state, block):
    memory, normal, stabilizer, segment_prev = state
    query_block, key_block, value_block, forget_block, input_block, segment_block = block
    block_len = query_block.shape[0]
    key_scale = 1.0 / math.sqrt(query_block.shape[2])
    cumulative = jnp.cumsum(forget_block, axis=1)
    positions = jnp.arange(block_len, dtype=jnp.int32)
    allowed = (positions[None, :] <= positions[:, None]) & (segment_block[None, :] == segment_block[:, None])
    log_weight = jnp.where(allowed[None], input_block[:, None, :] + cumulative[:, :, None] - cumulative[:, None, :], very_negative)
    linked = segment_block == segment_prev
    carried = jnp.where(linked[None, :], stabilizer[:, None] + cumulative, very_negative)
    row_max = jnp.maximum(lax.optimization_barrier(jnp.max(log_weight, axis=2)), carried)
    query_float = query_block.astype(jnp.float32)
    key_float = key_block.astype(jnp.float32)
    value_float = value_block.astype(jnp.float32)
    scores = jnp.einsum('thd,shd->hts', query_float, key_float, precision=lax.Precision.HIGHEST) * key_scale
    weights = scores * jnp.exp(log_weight - row_max[:, :, None])
    weights_low = lax.optimization_barrier(weights.astype(jnp.bfloat16)).astype(jnp.float32)
    reach_share = jnp.exp(carried - row_max)
    scaled_query = query_float * key_scale
    from_memory = jnp.einsum('thd,hdv->thv', scaled_query, memory, precision=lax.Precision.HIGHEST)
    from_normal = jnp.einsum('thd,hd->ht', scaled_query, normal, precision=lax.Precision.HIGHEST)
    numerator = jnp.einsum('hts,shv->thv', weights_low, value_float, precision=lax.Precision.HIGHEST)
    numerator = numerator + reach_share.T[:, :, None] * from_memory
    denominator = lax.optimization_barrier(jnp.sum(weights, axis=2)) + reach_share * from_normal
    segment_last = segment_block[block_len - 1]
    tail_weight = jnp.where((segment_block == segment_last)[None, :], input_block + cumulative[:, -1:] - cumulative, very_negative)
    tail_carry = jnp.where(segment_prev == segment_last, stabilizer + cumulative[:, -1], very_negative)
    stabilizer_new = jnp.maximum(lax.optimization_barrier(jnp.max(tail_weight, axis=1)), tail_carry)
    factor = jnp.exp(tail_weight - stabilizer_new[:, None])
    weighted_keys = key_float * factor.T[:, :, None]
    keys_low = lax.optimization_barrier(weighted_keys.astype(jnp.bfloat16)).astype(jnp.float32)
    decay_share = jnp.exp(tail_carry - stabilizer_new)
    memory_new = decay_share[:, None, None] * memory + jnp.einsum('shd,shv->hdv', keys_low, value_float, precision=lax.Precision.HIGHEST)
    normal_new = decay_share[:, None] * normal + lax.optimization_barrier(jnp.sum(weighted_keys, axis=0))
    return ((memory_new, normal_new, stabilizer_new, segment_last), (numerator, denominator, row_max))

def reference(query_input, key_input, value_input, kernel_taps, input_gate, forget_gate, request_lengths, output_weight):
    total_rows = query_input.shape[0]
    starts = (jnp.cumsum(request_lengths) - request_lengths).astype(jnp.int32)
    positions = jnp.arange(total_rows, dtype=jnp.int32)
    segments = (lax.optimization_barrier(jnp.sum((starts[None, :] <= positions[:, None]).astype(jnp.int32), axis=1)) - 1).astype(jnp.int32)
    query_conv = conv_silu(query_input, kernel_taps[0], segments)
    key_conv = conv_silu(key_input, kernel_taps[1], segments)
    block_len = min(512, TOK_DEV)
    block_count = total_rows // block_len
    log_forget = jax.nn.log_sigmoid(forget_gate)
    blocks = (query_conv.reshape(block_count, block_len, HEADS, DQK), key_conv.reshape(block_count, block_len, HEADS, DQK), value_input.reshape(block_count, block_len, HEADS, DV), log_forget.reshape(HEADS, block_count, block_len).transpose(1, 0, 2), input_gate.reshape(HEADS, block_count, block_len).transpose(1, 0, 2), segments.reshape(block_count, block_len))
    initial = (jnp.zeros((HEADS, DQK, DV), jnp.float32), jnp.zeros((HEADS, DQK), jnp.float32), jnp.full((HEADS,), very_negative, jnp.float32), jnp.array(-1, jnp.int32))
    _, (numerator, denominator, row_max) = lax.scan(block_pass, initial, blocks)
    floor_value = jnp.maximum(jnp.abs(denominator), 1.0).transpose(0, 2, 1)
    head_out = (numerator / floor_value[..., None]).reshape(total_rows, HEADS * DV).astype(jnp.bfloat16)
    return jnp.dot(head_out, output_weight, preferred_element_type=jnp.float32).astype(jnp.bfloat16)
```

```python
import functools

import jax
import jax.numpy as jnp
from jax import lax
from jax.experimental import pallas as pl
from jax.experimental.pallas import tpu as pltpu
from jax.sharding import PartitionSpec as P

MESH = pl.DeviceIdType.MESH
NEG = -1e30
SIDE = 8
F32 = jnp.float32
BF16 = jnp.bfloat16


def kernel(
    shards,
    chips,
    len_ref,
    q_ref,
    k_ref,
    v_ref,
    taps_ref,
    ig_ref,
    fg_ref,
    wo_hbm,
    out_ref,
    wo_ref,
    ext_ref,
    halo_send,
    halo_recv,
    scal_ref,
    stab_rows,
    thr_rows,
    m_rows,
    a_rows,
    b_rows,
    own_tiles,
    got_tiles,
    back_tiles,
    mem_tiles,
    norm_z,
    norm_y,
    num_ref,
    pair_send,
    pair_recv,
    x_send,
    x_recv,
    wo_sem,
    halo_sem,
    scal_sem,
    norm_sem,
    tile_sem,
    pair_ssem,
    pair_rsem,
    x_ssem,
    x_rsem,
):
    tokens, width = q_ref.shape
    values = v_ref.shape[1]
    scale = 1.0 / (width**0.5)
    me = lax.axis_index("seq")
    head = lax.axis_index("head")
    my_y, my_z = me // SIDE, me % SIDE
    my_x, my_c = head // 2, head % 2
    rows = shards // SIDE

    def seq_at(index):
        return {"seq": index}

    def head_at(index):
        return {"head": index}

    def remote(src, dst, ssem, rsem, where):
        return pltpu.make_async_remote_copy(
            src_ref=src, dst_ref=dst, send_sem=ssem, recv_sem=rsem, device_id=where, device_id_type=MESH
        )

    wo_copy = pltpu.make_async_copy(wo_hbm, wo_ref, wo_sem)
    wo_copy.start()

    barrier = pltpu.get_barrier_semaphore()

    def greet(step, carry):
        pl.semaphore_signal(
            barrier, inc=1, device_id=seq_at((me + step) % shards), device_id_type=MESH
        )
        return carry

    lax.fori_loop(1, shards, greet, 0)
    partner = 2 * my_x + (1 - my_c)
    pl.semaphore_signal(barrier, inc=1, device_id=head_at(partner), device_id_type=MESH)
    for step in range(1, chips):
        pl.semaphore_signal(
            barrier,
            inc=1,
            device_id=head_at(2 * ((my_x + step) % chips) + my_c),
            device_id_type=MESH,
        )

    offset = me * tokens
    starts = [jnp.int32(0)]
    for r in range(len_ref.shape[0] - 1):
        starts.append(starts[-1] + len_ref[r])

    def request_start(position):
        found = jnp.zeros_like(position)
        for start in starts[1:]:
            found = jnp.where(start <= position, start, found)
        return found

    t_col = lax.broadcasted_iota(jnp.int32, (tokens, 128), 0)
    begin_col = request_start(t_col + offset) - offset
    s_row = lax.broadcasted_iota(jnp.int32, (1, tokens), 1)
    last_begin = jnp.int32(0)
    for start in starts[1:]:
        last_begin = jnp.where(start <= offset + (tokens - 1), start, last_begin)
    last_begin = last_begin - offset

    fg = fg_ref[...]
    ig = ig_ref[...]
    log_forget = -(jnp.maximum(-fg, 0.0) + jnp.log1p(jnp.exp(-jnp.abs(fg))))
    hi = log_forget.astype(BF16)
    rest = log_forget - hi.astype(F32)
    mid = rest.astype(BF16)
    low = (rest - mid.astype(F32)).astype(BF16)
    pieces = jnp.concatenate(
        [hi.astype(F32), mid.astype(F32), low.astype(F32), jnp.zeros((5, tokens), F32)], axis=0
    ).astype(BF16)
    t_full = lax.broadcasted_iota(jnp.int32, (tokens, tokens), 0)
    s_full = lax.broadcasted_iota(jnp.int32, (tokens, tokens), 1)
    upper = jnp.where(t_full <= s_full, 1.0, 0.0).astype(BF16)
    cum_row = jnp.sum(
        jnp.dot(pieces, upper, preferred_element_type=F32), axis=0, keepdims=True
    )
    cum_last = cum_row[:, tokens - 1 : tokens]
    gain_row = ig - cum_row
    tail_row = jnp.where(s_row >= last_begin, gain_row + cum_last, NEG)
    stab = jnp.max(tail_row, axis=1, keepdims=True)
    factor_row = jnp.exp(tail_row - stab)
    through = jnp.where(last_begin < 0, cum_last, NEG)
    scal_ref[me] = jnp.concatenate(
        [jnp.broadcast_to(stab, (1, 128)), jnp.broadcast_to(through, (1, 128))], axis=0
    )
    turned = jnp.transpose(
        jnp.concatenate([cum_row, factor_row, jnp.zeros((126, tokens), F32)], axis=0)
    )
    cum_col = turned[:, 0:1]
    factor_col = turned[:, 1:2]

    halo_send[0] = k_ref[tokens - 16 : tokens, :]
    halo_send[1] = q_ref[tokens - 16 : tokens, :]

    pl.semaphore_wait(barrier, shards - 1 + chips)

    halo = remote(
        halo_send, halo_recv, halo_sem.at[0], halo_sem.at[1], seq_at((me + 1) % shards)
    )
    halo.start()

    def z_peer(step):
        return my_y * SIDE + (my_z + step) % SIDE

    def y_peer(step):
        return ((my_y + step) % rows) * SIDE + my_z

    for step in range(1, SIDE):
        remote(
            scal_ref.at[me], scal_ref.at[me], scal_sem.at[0], scal_sem.at[1], seq_at(z_peer(step))
        ).start()

    def conv_silu(source, which, tail):
        ext_ref[0:8, :] = halo_recv[tail, 8:16, :].astype(F32)
        ext_ref[8 : 8 + tokens, :] = source[...].astype(F32)
        running = taps_ref[which, 0:1, :] * ext_ref[8 : 8 + tokens, :]
        for lag in range(1, taps_ref.shape[1]):
            keep = (t_col - lag) >= begin_col
            keep = jnp.concatenate([keep.astype(F32)] * (width // 128), axis=1) > 0.0
            shifted = ext_ref[8 - lag : 8 - lag + tokens, :]
            running = running + jnp.where(keep, taps_ref[which, lag : lag + 1, :] * shifted, 0.0)
        return (running / (1.0 + jnp.exp(-running))).astype(BF16)

    halo.wait_recv()
    key = conv_silu(k_ref, 1, 0)
    weighted = key.astype(F32) * factor_col
    value = v_ref[...]
    memory = lax.dot_general(
        weighted.astype(BF16), value, (((0,), (0,)), ((), ())), preferred_element_type=F32
    ).astype(BF16)
    tile_rows = width // 16
    for c in range(values // 128):
        own_tiles[c * tile_rows : (c + 1) * tile_rows] = memory[
            :, c * 128 : (c + 1) * 128
        ].reshape(tile_rows, 16, 128)
    normal = jnp.sum(weighted, axis=0, keepdims=True)
    norm_z[my_z] = jnp.concatenate([normal[:, 0:128], normal[:, 128:256]], axis=0)

    def send_tile(step, carry):
        peer = (me + step) % shards
        remote(
            own_tiles.at[peer], got_tiles.at[me], tile_sem.at[0], tile_sem.at[1], seq_at(peer)
        ).start()
        return carry

    some = pl.ds(0, SIDE - 1)
    remote(
        scal_ref.at[some], scal_ref.at[some], scal_sem.at[0], scal_sem.at[1], seq_at(me)
    ).wait_recv()
    mine = pl.ds(my_y * SIDE, SIDE)
    for step in range(1, rows):
        remote(
            scal_ref.at[mine],
            scal_ref.at[mine],
            scal_sem.at[2],
            scal_sem.at[3],
            seq_at(y_peer(step)),
        ).start()
    lax.fori_loop(1, shards, send_tile, 0)
    for step in range(1, SIDE):
        remote(
            norm_z.at[my_z], norm_z.at[my_z], norm_sem.at[0], norm_sem.at[1], seq_at(z_peer(step))
        ).start()
    got_tiles[me] = own_tiles[me]

    query = conv_silu(q_ref, 0, 1)
    scores = (
        lax.dot_general(query, key, (((1,), (1,)), ((), ())), preferred_element_type=F32) * scale
    )

    most = pl.ds(0, (rows - 1) * SIDE)
    remote(
        scal_ref.at[most], scal_ref.at[most], scal_sem.at[2], scal_sem.at[3], seq_at(me)
    ).wait_recv()
    level = jnp.full((1, 128), NEG, F32)
    for s in range(shards):
        pair = scal_ref[s]
        stab_s, thr_s = pair[0:1, :], pair[1:2, :]
        m_rows[s : s + 1, :] = level
        carried_on = level + thr_s
        level = jnp.maximum(stab_s, carried_on)
        stab_rows[s : s + 1, :] = stab_s - level
        thr_rows[s : s + 1, :] = carried_on - level
    a_rows[...] = jnp.exp(thr_rows[...])
    b_rows[...] = jnp.exp(stab_rows[...])

    some_norm = pl.ds(0, SIDE - 1)
    remote(
        norm_z.at[some_norm], norm_z.at[some_norm], norm_sem.at[0], norm_sem.at[1], seq_at(me)
    ).wait_recv()
    total = jnp.zeros((2, 128), F32)
    for z in range(SIDE):
        at = pl.ds(my_y * SIDE + z, 1)
        total = a_rows[at, :] * total + b_rows[at, :] * norm_z[z]
    norm_y[my_y] = total
    for step in range(1, rows):
        remote(
            norm_y.at[my_y], norm_y.at[my_y], norm_sem.at[2], norm_sem.at[3], seq_at(y_peer(step))
        ).start()

    m_in = m_rows[pl.ds(me, 1), :][:, 0:1]
    begin_full = jnp.concatenate([begin_col] * (tokens // 128), axis=1)
    allowed = (s_full <= t_full) & (s_full >= begin_full)
    log_weight = jnp.where(allowed, gain_row + cum_col, NEG)
    carried = jnp.where(begin_col[:, 0:1] < 0, m_in + cum_col, NEG)
    row_max = jnp.maximum(jnp.max(log_weight, axis=1, keepdims=True), carried)
    weights = scores * jnp.exp(log_weight - row_max)
    reach = jnp.exp(carried - row_max) * scale
    num_ref[...] = jnp.dot(weights.astype(BF16), value, preferred_element_type=F32)
    den_inside = jnp.sum(weights, axis=1, keepdims=True)

    most_tiles = pl.ds(0, shards - 1)
    remote(
        got_tiles.at[most_tiles],
        got_tiles.at[most_tiles],
        tile_sem.at[0],
        tile_sem.at[1],
        seq_at(me),
    ).wait_recv()
    state = jnp.zeros((16, 128), F32)
    for s in range(shards):
        back_tiles[s] = state.astype(BF16)
        state = a_rows[s : s + 1, :] * state + b_rows[s : s + 1, :] * got_tiles[s].astype(F32)

    def send_back(step, carry):
        peer = (me + step) % shards
        remote(
            back_tiles.at[peer], mem_tiles.at[me], tile_sem.at[2], tile_sem.at[3], seq_at(peer)
        ).start()
        return carry

    lax.fori_loop(1, shards, send_back, 0)
    mem_tiles[me] = back_tiles[me]

    some_y = pl.ds(0, rows - 1)
    remote(
        norm_y.at[some_y], norm_y.at[some_y], norm_sem.at[2], norm_sem.at[3], seq_at(me)
    ).wait_recv()
    norm_in = jnp.zeros((2, 128), F32)
    for y in range(rows):
        decay = a_rows[y * SIDE : y * SIDE + 1, :]
        for z in range(1, SIDE):
            decay = decay * a_rows[y * SIDE + z : y * SIDE + z + 1, :]
        norm_in = jnp.where(y < my_y, decay * norm_in + norm_y[y], norm_in)
    for z in range(SIDE):
        at = pl.ds(my_y * SIDE + z, 1)
        norm_in = jnp.where(
            z < my_z, a_rows[at, :] * norm_in + b_rows[at, :] * norm_z[z], norm_in
        )
    norm_row = jnp.concatenate([norm_in[0:1, :], norm_in[1:2, :]], axis=1)
    from_normal = jnp.sum(query.astype(F32) * norm_row, axis=1, keepdims=True)
    floor = jnp.maximum(jnp.abs(den_inside + reach * from_normal), 1.0)
    inverse = 1.0 / floor

    wo_copy.wait()
    remote(
        mem_tiles.at[most_tiles],
        mem_tiles.at[most_tiles],
        tile_sem.at[2],
        tile_sem.at[3],
        seq_at(me),
    ).wait_recv()
    parts = []
    for c in range(values // 128):
        block = mem_tiles[c * tile_rows : (c + 1) * tile_rows].reshape(width, 128)
        from_memory = jnp.dot(query, block, preferred_element_type=F32)
        at = slice(c * 128, (c + 1) * 128)
        parts.append(((num_ref[:, at] + reach * from_memory) * inverse).astype(BF16))
    head_out = jnp.concatenate(parts, axis=1)

    out_cols = out_ref.shape[1]

    def project(x, core):
        column = pl.multiple_of((2 * x + core) * out_cols, out_cols)
        return jnp.dot(head_out, wo_ref[:, pl.ds(column, out_cols)], preferred_element_type=F32)

    order = [1, 2, 3, 0] if chips == 4 else list(range(1, chips)) + [0]
    pair_copies = {}
    for step in order:
        pair_send[step] = project((my_x + step) % chips, 1 - my_c).astype(BF16)
        pair_copies[step] = remote(
            pair_send.at[step],
            pair_recv.at[step],
            pair_ssem.at[step],
            pair_rsem.at[step],
            head_at(partner),
        )
        pair_copies[step].start()
    x_copies = []
    for step in order:
        ours = project((my_x + step) % chips, my_c)
        pair_copies[step].wait_recv()
        both = ours + pair_recv[step].astype(F32)
        if step:
            x_send[step - 1] = both.astype(BF16)
            copy = remote(
                x_send.at[step - 1],
                x_recv.at[step - 1],
                x_ssem.at[step - 1],
                x_rsem.at[step - 1],
                head_at(2 * ((my_x + step) % chips) + my_c),
            )
            copy.start()
            x_copies.append(copy)
    for step, copy in enumerate(x_copies):
        copy.wait_recv()
        both = both + x_recv[step].astype(F32)
    out_ref[...] = both.astype(BF16)

    halo.wait_send()
    remote(
        scal_ref.at[some], scal_ref.at[some], scal_sem.at[0], scal_sem.at[1], seq_at(me)
    ).wait_send()
    remote(
        scal_ref.at[most], scal_ref.at[most], scal_sem.at[2], scal_sem.at[3], seq_at(me)
    ).wait_send()
    remote(
        norm_z.at[some_norm], norm_z.at[some_norm], norm_sem.at[0], norm_sem.at[1], seq_at(me)
    ).wait_send()
    remote(
        norm_y.at[some_y], norm_y.at[some_y], norm_sem.at[2], norm_sem.at[3], seq_at(me)
    ).wait_send()
    for first, tiles in ((0, own_tiles), (2, back_tiles)):
        remote(
            tiles.at[most_tiles],
            tiles.at[most_tiles],
            tile_sem.at[first],
            tile_sem.at[first + 1],
            seq_at(me),
        ).wait_send()
    for copy in list(pair_copies.values()) + x_copies:
        copy.wait_send()


def on_device(
    shards,
    chips,
    query_input,
    key_input,
    value_input,
    kernel_taps,
    input_gate,
    forget_gate,
    request_lengths,
    output_weight,
):
    tokens, width = query_input.shape
    values = value_input.shape[1]
    out_cols = output_weight.shape[1] // (2 * chips)
    vmem = pl.BlockSpec(memory_space=pltpu.VMEM)
    dma = pltpu.SemaphoreType.DMA
    return pl.pallas_call(
        functools.partial(kernel, shards, chips),
        out_shape=jax.ShapeDtypeStruct((tokens, out_cols), BF16),
        in_specs=[pl.BlockSpec(memory_space=pltpu.SMEM)]
        + [vmem] * 6
        + [pl.BlockSpec(memory_space=pl.ANY)],
        out_specs=vmem,
        scratch_shapes=[
            pltpu.VMEM(output_weight.shape, BF16),
            pltpu.VMEM((tokens + 8, width), F32),
            pltpu.VMEM((2, 16, width), BF16),
            pltpu.VMEM((2, 16, width), BF16),
            pltpu.VMEM((shards, 2, 128), F32),
            pltpu.VMEM((shards, 128), F32),
            pltpu.VMEM((shards, 128), F32),
            pltpu.VMEM((shards, 128), F32),
            pltpu.VMEM((shards, 128), F32),
            pltpu.VMEM((shards, 128), F32),
            pltpu.VMEM((shards, 16, 128), BF16),
            pltpu.VMEM((shards, 16, 128), BF16),
            pltpu.VMEM((shards, 16, 128), BF16),
            pltpu.VMEM((shards, 16, 128), BF16),
            pltpu.VMEM((SIDE, 2, 128), F32),
            pltpu.VMEM((shards // SIDE, 2, 128), F32),
            pltpu.VMEM((tokens, values), F32),
            pltpu.VMEM((chips, tokens, out_cols), BF16),
            pltpu.VMEM((chips, tokens, out_cols), BF16),
            pltpu.VMEM((chips - 1, tokens, out_cols), BF16),
            pltpu.VMEM((chips - 1, tokens, out_cols), BF16),
            dma,
            dma((2,)),
            dma((4,)),
            dma((4,)),
            dma((4,)),
            dma((chips,)),
            dma((chips,)),
            dma((chips - 1,)),
            dma((chips - 1,)),
        ],
        compiler_params=pltpu.CompilerParams(
            collective_id=0, has_side_effects=True, vmem_limit_bytes=40 << 20
        ),
    )(
        request_lengths,
        query_input,
        key_input,
        value_input,
        kernel_taps,
        input_gate,
        forget_gate,
        output_weight,
    )


def solution(mesh):
    placed = (
        P("seq", "head"),
        P("seq", "head"),
        P("seq", "head"),
        P(None, None, "head"),
        P("head", "seq"),
        P("head", "seq"),
        P(),
        P("head", None),
    )
    return jax.shard_map(
        functools.partial(on_device, mesh.shape["seq"], mesh.shape["head"] // 2),
        mesh=mesh,
        in_specs=placed,
        out_specs=P("seq", "head"),
        check_vma=False,
    )
```

```python
import functools

import jax
import jax.numpy as jnp
from jax import lax
from jax.experimental import pallas as pl
from jax.experimental.pallas import tpu as pltpu
from jax.sharding import PartitionSpec as P

MESH = pl.DeviceIdType.MESH
NEG = -1e30
SIDE = 8
F32 = jnp.float32
BF16 = jnp.bfloat16


def kernel(
    shards,
    chips,
    len_hbm,
    q_hbm,
    k_hbm,
    v_hbm,
    taps_hbm,
    ig_hbm,
    fg_hbm,
    wo_hbm,
    out_ref,
    len_ref,
    q_ref,
    k_ref,
    v_ref,
    taps_ref,
    ig_ref,
    fg_ref,
    wo_ref,
    ext_ref,
    halo_recv,
    scal_ref,
    stab_rows,
    thr_rows,
    m_rows,
    a_rows,
    b_rows,
    own_tiles,
    got_tiles,
    back_tiles,
    mem_tiles,
    norm_z,
    norm_y,
    num_ref,
    pair_send,
    pair_recv,
    x_send,
    x_recv,
    load_sem,
    halo_sem,
    scal_sem,
    norm_sem,
    tile_sem,
    pair_ssem,
    pair_rsem,
    x_ssem,
    x_rsem,
    rows_sem,
):
    tokens, width = q_hbm.shape
    values = v_hbm.shape[1]
    scale = 1.0 / (width**0.5)
    me = lax.axis_index("seq")
    head = lax.axis_index("head")
    my_y, my_z = me // SIDE, me % SIDE
    my_x, my_c = head // 2, head % 2
    rows = shards // SIDE

    def seq_at(index):
        return {"seq": index}

    def head_at(index):
        return {"head": index}

    def remote(src, dst, ssem, rsem, where):
        return pltpu.make_async_remote_copy(
            src_ref=src, dst_ref=dst, send_sem=ssem, recv_sem=rsem, device_id=where, device_id_type=MESH
        )

    loads = [
        pltpu.make_async_copy(src, dst, load_sem.at[i])
        for i, (src, dst) in enumerate(
            (
                (fg_hbm, fg_ref),
                (ig_hbm, ig_ref),
                (k_hbm, k_ref),
                (q_hbm, q_ref),
                (taps_hbm, taps_ref),
                (v_hbm, v_ref),
                (wo_hbm, wo_ref),
                (len_hbm, len_ref),
            )
        )
    ]
    for load in loads:
        load.start()

    barrier = pltpu.get_barrier_semaphore()

    def z_peer(step):
        return my_y * SIDE + (my_z + step) % SIDE

    def y_peer(step):
        return ((my_y + step) % rows) * SIDE + my_z

    partner = 2 * my_x + (1 - my_c)
    x_next = 2 * ((my_x + 1) % chips) + my_c
    x_prev = 2 * ((my_x + chips - 1) % chips) + my_c
    known = [seq_at((me + shards - 1) % shards)]
    known += [seq_at(z_peer(step)) for step in (4, 3, 5, 2, 6, 1, 7)]
    known += [seq_at(y_peer(step)) for step in (4, 3, 5, 2, 6, 1, 7)]
    known += [head_at(partner), head_at(x_next), head_at(x_prev)]
    for where in known:
        pl.semaphore_signal(barrier, inc=1, device_id=where, device_id_type=MESH)

    loads[7].wait()
    offset = me * tokens
    starts = [jnp.int32(0)]
    for r in range(len_ref.shape[0] - 1):
        starts.append(starts[-1] + len_ref[r])

    def request_start(position):
        found = jnp.zeros_like(position)
        for start in starts[1:]:
            found = jnp.where(start <= position, start, found)
        return found

    t_col = lax.broadcasted_iota(jnp.int32, (tokens, 128), 0)
    begin_col = request_start(t_col + offset) - offset
    s_row = lax.broadcasted_iota(jnp.int32, (1, tokens), 1)
    last_begin = jnp.int32(0)
    for start in starts[1:]:
        last_begin = jnp.where(start <= offset + (tokens - 1), start, last_begin)
    last_begin = last_begin - offset

    loads[0].wait()
    loads[1].wait()
    fg = fg_ref[...]
    ig = ig_ref[...]
    log_forget = -(jnp.maximum(-fg, 0.0) + jnp.log1p(jnp.exp(-jnp.abs(fg))))
    hi = log_forget.astype(BF16)
    rest = log_forget - hi.astype(F32)
    mid = rest.astype(BF16)
    low = (rest - mid.astype(F32)).astype(BF16)
    pieces = jnp.concatenate(
        [hi.astype(F32), mid.astype(F32), low.astype(F32), jnp.zeros((5, tokens), F32)], axis=0
    ).astype(BF16)
    t_full = lax.broadcasted_iota(jnp.int32, (tokens, tokens), 0)
    s_full = lax.broadcasted_iota(jnp.int32, (tokens, tokens), 1)
    upper = jnp.where(t_full <= s_full, 1.0, 0.0).astype(BF16)
    cum_row = jnp.sum(
        jnp.dot(pieces, upper, preferred_element_type=F32), axis=0, keepdims=True
    )
    cum_last = cum_row[:, tokens - 1 : tokens]
    gain_row = ig - cum_row
    tail_row = jnp.where(s_row >= last_begin, gain_row + cum_last, NEG)
    stab = jnp.max(tail_row, axis=1, keepdims=True)
    factor_row = jnp.exp(tail_row - stab)
    through = jnp.where(last_begin < 0, cum_last, NEG)
    scal_ref[me] = jnp.concatenate(
        [jnp.broadcast_to(stab, (1, 128)), jnp.broadcast_to(through, (1, 128))], axis=0
    )
    turned = jnp.transpose(
        jnp.concatenate([cum_row, factor_row, jnp.zeros((126, tokens), F32)], axis=0)
    )
    cum_col = turned[:, 0:1]
    factor_col = turned[:, 1:2]

    loads[2].wait()
    loads[3].wait()
    pl.semaphore_wait(barrier, len(known))

    tail = pl.ds(tokens - 16, 16)
    follower = seq_at((me + 1) % shards)
    halos = [
        remote(ref.at[tail, :], halo_recv.at[i], halo_sem.at[2 * i], halo_sem.at[2 * i + 1], follower)
        for i, ref in enumerate((k_ref, q_ref))
    ]
    halos[0].start()
    for step in (4, 3, 5, 2, 6, 1, 7):
        pl.semaphore_signal(
            rows_sem, inc=1, device_id=seq_at(y_peer(step)), device_id_type=MESH
        )
    for step in (4, 3, 5, 2, 6, 1, 7):
        remote(
            scal_ref.at[me], scal_ref.at[me], scal_sem.at[0], scal_sem.at[1], seq_at(z_peer(step))
        ).start()
    halos[1].start()

    def conv_silu(which, first, count):
        begin = begin_col[first : first + count]
        position = t_col[first : first + count]
        running = taps_ref[which, 0:1, :] * ext_ref[8 + first : 8 + first + count, :]
        for lag in range(1, taps_ref.shape[1]):
            keep = (position - lag) >= begin
            keep = jnp.concatenate([keep.astype(F32)] * (width // 128), axis=1) > 0.0
            shifted = ext_ref[8 + first - lag : 8 + first - lag + count, :]
            running = running + jnp.where(keep, taps_ref[which, lag : lag + 1, :] * shifted, 0.0)
        return (running / (1.0 + jnp.exp(-running))).astype(BF16)

    def outer_sum(left, right):
        return lax.dot_general(
            left, right, (((0,), (0,)), ((), ())), preferred_element_type=F32
        )

    loads[4].wait()
    loads[5].wait()
    ext_ref[8 : 8 + tokens, :] = k_ref[...].astype(F32)
    key_rest = conv_silu(1, 16, tokens - 16)
    weighted_rest = key_rest.astype(F32) * factor_col[16:]
    memory_rest = outer_sum(weighted_rest.astype(BF16), v_ref[16:, :])
    normal_rest = jnp.sum(weighted_rest, axis=0, keepdims=True)
    halos[0].wait_recv()
    ext_ref[0:8, :] = halo_recv[0, 8:16, :].astype(F32)
    key_first = conv_silu(1, 0, 16)
    weighted_first = key_first.astype(F32) * factor_col[:16]
    memory = (memory_rest + outer_sum(weighted_first.astype(BF16), v_ref[:16, :])).astype(BF16)
    key = jnp.concatenate([key_first, key_rest], axis=0)
    value = v_ref[...]
    tile_rows = width // 16
    for c in range(values // 128):
        own_tiles[c * tile_rows : (c + 1) * tile_rows] = memory[
            :, c * 128 : (c + 1) * 128
        ].reshape(tile_rows, 16, 128)
    normal = normal_rest + jnp.sum(weighted_first, axis=0, keepdims=True)
    norm_z[my_z] = jnp.concatenate([normal[:, 0:128], normal[:, 128:256]], axis=0)

    def far(step):
        dy, dz = step // SIDE, step % SIDE
        return -(min(dy, rows - dy) + min(dz, SIDE - dz))

    steps = sorted(range(1, shards), key=far)

    def peer_at(step):
        return ((my_y + step // SIDE) % rows) * SIDE + (my_z + step % SIDE) % SIDE

    def send_tiles(chosen):
        for step in chosen:
            peer = peer_at(step)
            remote(
                own_tiles.at[peer], got_tiles.at[me], tile_sem.at[0], tile_sem.at[1], seq_at(peer)
            ).start()

    pl.semaphore_wait(rows_sem, rows - 1)
    send_tiles(steps[:24])

    some = pl.ds(0, SIDE - 1)
    remote(
        scal_ref.at[some], scal_ref.at[some], scal_sem.at[0], scal_sem.at[1], seq_at(me)
    ).wait_recv()
    mine = pl.ds(my_y * SIDE, SIDE)
    for step in range(1, rows):
        remote(
            scal_ref.at[mine],
            scal_ref.at[mine],
            scal_sem.at[2],
            scal_sem.at[3],
            seq_at(y_peer(step)),
        ).start()
    send_tiles(steps[24:])
    for step in range(1, SIDE):
        remote(
            norm_z.at[my_z], norm_z.at[my_z], norm_sem.at[0], norm_sem.at[1], seq_at(z_peer(step))
        ).start()
    got_tiles[me] = own_tiles[me]

    halos[1].wait_recv()
    ext_ref[0:8, :] = halo_recv[1, 8:16, :].astype(F32)
    ext_ref[8 : 8 + tokens, :] = q_ref[...].astype(F32)
    query = conv_silu(0, 0, tokens)
    scores = (
        lax.dot_general(query, key, (((1,), (1,)), ((), ())), preferred_element_type=F32) * scale
    )

    most = pl.ds(0, (rows - 1) * SIDE)
    remote(
        scal_ref.at[most], scal_ref.at[most], scal_sem.at[2], scal_sem.at[3], seq_at(me)
    ).wait_recv()
    level = jnp.full((1, 128), NEG, F32)
    for s in range(shards):
        pair = scal_ref[s]
        stab_s, thr_s = pair[0:1, :], pair[1:2, :]
        m_rows[s : s + 1, :] = level
        carried_on = level + thr_s
        level = jnp.maximum(stab_s, carried_on)
        stab_rows[s : s + 1, :] = stab_s - level
        thr_rows[s : s + 1, :] = carried_on - level
    a_rows[...] = jnp.exp(thr_rows[...])
    b_rows[...] = jnp.exp(stab_rows[...])

    some_norm = pl.ds(0, SIDE - 1)
    remote(
        norm_z.at[some_norm], norm_z.at[some_norm], norm_sem.at[0], norm_sem.at[1], seq_at(me)
    ).wait_recv()
    total = jnp.zeros((2, 128), F32)
    for z in range(SIDE):
        at = pl.ds(my_y * SIDE + z, 1)
        total = a_rows[at, :] * total + b_rows[at, :] * norm_z[z]
    norm_y[my_y] = total
    for step in range(1, rows):
        remote(
            norm_y.at[my_y], norm_y.at[my_y], norm_sem.at[2], norm_sem.at[3], seq_at(y_peer(step))
        ).start()

    m_in = m_rows[pl.ds(me, 1), :][:, 0:1]
    begin_full = jnp.concatenate([begin_col] * (tokens // 128), axis=1)
    allowed = (s_full <= t_full) & (s_full >= begin_full)
    log_weight = jnp.where(allowed, gain_row + cum_col, NEG)
    carried = jnp.where(begin_col[:, 0:1] < 0, m_in + cum_col, NEG)
    row_max = jnp.maximum(jnp.max(log_weight, axis=1, keepdims=True), carried)
    weights = scores * jnp.exp(log_weight - row_max)
    reach = jnp.exp(carried - row_max) * scale
    num_ref[...] = jnp.dot(weights.astype(BF16), value, preferred_element_type=F32)
    den_inside = jnp.sum(weights, axis=1, keepdims=True)

    most_tiles = pl.ds(0, shards - 1)
    remote(
        got_tiles.at[most_tiles],
        got_tiles.at[most_tiles],
        tile_sem.at[0],
        tile_sem.at[1],
        seq_at(me),
    ).wait_recv()
    state = jnp.zeros((16, 128), F32)
    for s in range(shards):
        back_tiles[s] = state.astype(BF16)
        state = a_rows[s : s + 1, :] * state + b_rows[s : s + 1, :] * got_tiles[s].astype(F32)

    for step in steps:
        peer = peer_at(step)
        remote(
            back_tiles.at[peer], mem_tiles.at[me], tile_sem.at[2], tile_sem.at[3], seq_at(peer)
        ).start()
    mem_tiles[me] = back_tiles[me]

    some_y = pl.ds(0, rows - 1)
    remote(
        norm_y.at[some_y], norm_y.at[some_y], norm_sem.at[2], norm_sem.at[3], seq_at(me)
    ).wait_recv()
    norm_in = jnp.zeros((2, 128), F32)
    for y in range(rows):
        decay = a_rows[y * SIDE : y * SIDE + 1, :]
        for z in range(1, SIDE):
            decay = decay * a_rows[y * SIDE + z : y * SIDE + z + 1, :]
        norm_in = jnp.where(y < my_y, decay * norm_in + norm_y[y], norm_in)
    for z in range(SIDE):
        at = pl.ds(my_y * SIDE + z, 1)
        norm_in = jnp.where(
            z < my_z, a_rows[at, :] * norm_in + b_rows[at, :] * norm_z[z], norm_in
        )
    norm_row = jnp.concatenate([norm_in[0:1, :], norm_in[1:2, :]], axis=1)
    from_normal = jnp.sum(query.astype(F32) * norm_row, axis=1, keepdims=True)
    floor = jnp.maximum(jnp.abs(den_inside + reach * from_normal), 1.0)
    inverse = 1.0 / floor

    loads[6].wait()
    remote(
        mem_tiles.at[most_tiles],
        mem_tiles.at[most_tiles],
        tile_sem.at[2],
        tile_sem.at[3],
        seq_at(me),
    ).wait_recv()
    parts = []
    for c in range(values // 128):
        block = mem_tiles[c * tile_rows : (c + 1) * tile_rows].reshape(width, 128)
        from_memory = jnp.dot(query, block, preferred_element_type=F32)
        at = slice(c * 128, (c + 1) * 128)
        parts.append(((num_ref[:, at] + reach * from_memory) * inverse).astype(BF16))
    head_out = jnp.concatenate(parts, axis=1)

    out_cols = out_ref.shape[1]
    half = tokens // 2

    def project(x, core):
        column = pl.multiple_of((2 * x + core) * out_cols, out_cols)
        return jnp.dot(head_out, wo_ref[:, pl.ds(column, out_cols)], preferred_element_type=F32)

    pair_copies = {}

    def pair_start(step):
        pair_send[step] = project((my_x + step) % chips, 1 - my_c).astype(BF16)
        pair_copies[step] = remote(
            pair_send.at[step],
            pair_recv.at[step],
            pair_ssem.at[step],
            pair_rsem.at[step],
            head_at(partner),
        )
        pair_copies[step].start()

    def chip_sum(step):
        ours = project((my_x + step) % chips, my_c)
        pair_copies[step].wait_recv()
        return ours + pair_recv[step].astype(F32)

    def x_copy(slot, where):
        return remote(
            x_send.at[slot], x_recv.at[slot], x_ssem.at[slot], x_rsem.at[slot], head_at(where)
        )

    x_copies = [x_copy(slot, x_next if slot % 2 == 0 else x_prev) for slot in range(6)]
    pair_start(2)
    pair_start(1)
    pair_start(3)
    pair_start(0)
    opposite = chip_sum(2)
    x_send[0] = opposite[:half].astype(BF16)
    x_copies[0].start()
    x_send[1] = opposite[half:].astype(BF16)
    x_copies[1].start()
    after = chip_sum(1)
    x_send[2] = after[half:].astype(BF16)
    x_copies[2].start()
    before = chip_sum(3)
    x_send[3] = before[:half].astype(BF16)
    x_copies[3].start()
    x_copies[0].wait_recv()
    x_send[4] = (after[:half] + x_recv[0].astype(F32)).astype(BF16)
    x_copies[4].start()
    x_copies[1].wait_recv()
    x_send[5] = (before[half:] + x_recv[1].astype(F32)).astype(BF16)
    x_copies[5].start()
    both = chip_sum(0)
    x_copies[3].wait_recv()
    x_copies[4].wait_recv()
    out_ref[:half] = (both[:half] + x_recv[3].astype(F32) + x_recv[4].astype(F32)).astype(BF16)
    x_copies[2].wait_recv()
    x_copies[5].wait_recv()
    out_ref[half:] = (both[half:] + x_recv[2].astype(F32) + x_recv[5].astype(F32)).astype(BF16)

    for copy in halos:
        copy.wait_send()
    remote(
        scal_ref.at[some], scal_ref.at[some], scal_sem.at[0], scal_sem.at[1], seq_at(me)
    ).wait_send()
    remote(
        scal_ref.at[most], scal_ref.at[most], scal_sem.at[2], scal_sem.at[3], seq_at(me)
    ).wait_send()
    remote(
        norm_z.at[some_norm], norm_z.at[some_norm], norm_sem.at[0], norm_sem.at[1], seq_at(me)
    ).wait_send()
    remote(
        norm_y.at[some_y], norm_y.at[some_y], norm_sem.at[2], norm_sem.at[3], seq_at(me)
    ).wait_send()
    for first, tiles in ((0, own_tiles), (2, back_tiles)):
        remote(
            tiles.at[most_tiles],
            tiles.at[most_tiles],
            tile_sem.at[first],
            tile_sem.at[first + 1],
            seq_at(me),
        ).wait_send()
    for copy in list(pair_copies.values()) + x_copies:
        copy.wait_send()


def on_device(
    shards,
    chips,
    query_input,
    key_input,
    value_input,
    kernel_taps,
    input_gate,
    forget_gate,
    request_lengths,
    output_weight,
):
    tokens, width = query_input.shape
    values = value_input.shape[1]
    out_cols = output_weight.shape[1] // (2 * chips)
    vmem = pl.BlockSpec(memory_space=pltpu.VMEM)
    dma = pltpu.SemaphoreType.DMA
    return pl.pallas_call(
        functools.partial(kernel, shards, chips),
        out_shape=jax.ShapeDtypeStruct((tokens, out_cols), BF16),
        in_specs=[pl.BlockSpec(memory_space=pltpu.HBM)] * 8,
        out_specs=vmem,
        scratch_shapes=[pltpu.SMEM(request_lengths.shape, jnp.int32)]
        + [
            pltpu.VMEM(a.shape, a.dtype)
            for a in (
                query_input,
                key_input,
                value_input,
                kernel_taps,
                input_gate,
                forget_gate,
            )
        ]
        + [
            pltpu.VMEM(output_weight.shape, BF16),
            pltpu.VMEM((tokens + 8, width), F32),
            pltpu.VMEM((2, 16, width), BF16),
            pltpu.VMEM((shards, 2, 128), F32),
            pltpu.VMEM((shards, 128), F32),
            pltpu.VMEM((shards, 128), F32),
            pltpu.VMEM((shards, 128), F32),
            pltpu.VMEM((shards, 128), F32),
            pltpu.VMEM((shards, 128), F32),
            pltpu.VMEM((shards, 16, 128), BF16),
            pltpu.VMEM((shards, 16, 128), BF16),
            pltpu.VMEM((shards, 16, 128), BF16),
            pltpu.VMEM((shards, 16, 128), BF16),
            pltpu.VMEM((SIDE, 2, 128), F32),
            pltpu.VMEM((shards // SIDE, 2, 128), F32),
            pltpu.VMEM((tokens, values), F32),
            pltpu.VMEM((chips, tokens, out_cols), BF16),
            pltpu.VMEM((chips, tokens, out_cols), BF16),
            pltpu.VMEM((6, tokens // 2, out_cols), BF16),
            pltpu.VMEM((6, tokens // 2, out_cols), BF16),
            dma((8,)),
            dma((4,)),
            dma((4,)),
            dma((4,)),
            dma((4,)),
            dma((chips,)),
            dma((chips,)),
            dma((6,)),
            dma((6,)),
            pltpu.SemaphoreType.REGULAR,
        ],
        compiler_params=pltpu.CompilerParams(
            collective_id=0, has_side_effects=True, vmem_limit_bytes=32 << 20
        ),
    )(
        *(
            pltpu.with_memory_space_constraint(a, pltpu.HBM)
            for a in (
                request_lengths,
                query_input,
                key_input,
                value_input,
                kernel_taps,
                input_gate,
                forget_gate,
                output_weight,
            )
        ),
    )


def solution(mesh):
    placed = (
        P("seq", "head"),
        P("seq", "head"),
        P("seq", "head"),
        P(None, None, "head"),
        P("head", "seq"),
        P("head", "seq"),
        P(),
        P("head", None),
    )
    return jax.shard_map(
        functools.partial(on_device, mesh.shape["seq"], mesh.shape["head"] // 2),
        mesh=mesh,
        in_specs=placed,
        out_specs=P("seq", "head"),
        check_vma=False,
    )
```

```python
import functools

import jax
import jax.numpy as jnp
from jax import lax
from jax.experimental import pallas as pl
from jax.experimental.pallas import tpu as pltpu
from jax.sharding import PartitionSpec as P

MESH = pl.DeviceIdType.MESH
NEG = -1e30
SIDE = 8
F32 = jnp.float32
BF16 = jnp.bfloat16


def kernel(
    shards,
    chips,
    len_hbm,
    q_hbm,
    k_hbm,
    v_hbm,
    taps_hbm,
    ig_hbm,
    fg_hbm,
    wo_hbm,
    out_ref,
    len_ref,
    q_ref,
    k_ref,
    v_ref,
    taps_ref,
    ig_ref,
    fg_ref,
    wo_ref,
    ext_ref,
    halo_recv,
    scal_ref,
    stab_rows,
    thr_rows,
    m_rows,
    a_rows,
    b_rows,
    own_tiles,
    got_tiles,
    back_tiles,
    mem_tiles,
    norm_z,
    norm_y,
    num_ref,
    pair_send,
    pair_recv,
    x_send,
    x_recv,
    load_sem,
    halo_sem,
    scal_sem,
    norm_sem,
    tile_sem,
    pair_ssem,
    pair_rsem,
    x_ssem,
    x_rsem,
    rows_sem,
):
    tokens, width = q_hbm.shape
    values = v_hbm.shape[1]
    scale = 1.0 / (width**0.5)
    me = lax.axis_index("seq")
    head = lax.axis_index("head")
    my_y, my_z = me // SIDE, me % SIDE
    my_x, my_c = head // 2, head % 2
    rows = shards // SIDE

    def seq_at(index):
        return {"seq": index}

    def head_at(index):
        return {"head": index}

    def remote(src, dst, ssem, rsem, where):
        return pltpu.make_async_remote_copy(
            src_ref=src, dst_ref=dst, send_sem=ssem, recv_sem=rsem, device_id=where, device_id_type=MESH
        )

    barrier = pltpu.get_barrier_semaphore()

    def z_peer(step):
        return my_y * SIDE + (my_z + step) % SIDE

    def y_peer(step):
        return ((my_y + step) % rows) * SIDE + my_z

    partner = 2 * my_x + (1 - my_c)
    x_next = 2 * ((my_x + 1) % chips) + my_c
    x_prev = 2 * ((my_x + chips - 1) % chips) + my_c
    known = [seq_at((me + shards - 1) % shards)]
    known += [seq_at(z_peer(step)) for step in (4, 3, 5, 2, 6, 1, 7)]
    known += [seq_at(y_peer(step)) for step in (4, 3, 5, 2, 6, 1, 7)]
    known += [head_at(partner), head_at(x_next), head_at(x_prev)]
    for where in known:
        pl.semaphore_signal(barrier, inc=1, device_id=where, device_id_type=MESH)

    loads = [
        pltpu.make_async_copy(src, dst, load_sem.at[i])
        for i, (src, dst) in enumerate(
            (
                (fg_hbm, fg_ref),
                (ig_hbm, ig_ref),
                (k_hbm, k_ref),
                (q_hbm, q_ref),
                (taps_hbm, taps_ref),
                (v_hbm, v_ref),
                (wo_hbm, wo_ref),
                (len_hbm, len_ref),
            )
        )
    ]
    for load in loads:
        load.start()

    loads[7].wait()
    offset = me * tokens
    starts = [jnp.int32(0)]
    for r in range(len_ref.shape[0] - 1):
        starts.append(starts[-1] + len_ref[r])

    def request_start(position):
        found = jnp.zeros_like(position)
        for start in starts[1:]:
            found = jnp.where(start <= position, start, found)
        return found

    t_col = lax.broadcasted_iota(jnp.int32, (tokens, 128), 0)
    begin_col = request_start(t_col + offset) - offset
    s_row = lax.broadcasted_iota(jnp.int32, (1, tokens), 1)
    last_begin = jnp.int32(0)
    for start in starts[1:]:
        last_begin = jnp.where(start <= offset + (tokens - 1), start, last_begin)
    last_begin = last_begin - offset

    loads[0].wait()
    loads[1].wait()
    fg = fg_ref[...]
    ig = ig_ref[...]
    log_forget = -(jnp.maximum(-fg, 0.0) + jnp.log1p(jnp.exp(-jnp.abs(fg))))
    hi = log_forget.astype(BF16)
    rest = log_forget - hi.astype(F32)
    mid = rest.astype(BF16)
    low = (rest - mid.astype(F32)).astype(BF16)
    pieces = jnp.concatenate(
        [hi.astype(F32), mid.astype(F32), low.astype(F32), jnp.zeros((5, tokens), F32)], axis=0
    ).astype(BF16)
    t_full = lax.broadcasted_iota(jnp.int32, (tokens, tokens), 0)
    s_full = lax.broadcasted_iota(jnp.int32, (tokens, tokens), 1)
    upper = jnp.where(t_full <= s_full, 1.0, 0.0).astype(BF16)
    cum_row = jnp.sum(
        jnp.dot(pieces, upper, preferred_element_type=F32), axis=0, keepdims=True
    )
    cum_last = cum_row[:, tokens - 1 : tokens]
    gain_row = ig - cum_row
    tail_row = jnp.where(s_row >= last_begin, gain_row + cum_last, NEG)
    stab = jnp.max(tail_row, axis=1, keepdims=True)
    factor_row = jnp.exp(tail_row - stab)
    through = jnp.where(last_begin < 0, cum_last, NEG)
    scal_ref[me] = jnp.concatenate(
        [jnp.broadcast_to(stab, (1, 128)), jnp.broadcast_to(through, (1, 128))], axis=0
    )
    turned = jnp.transpose(
        jnp.concatenate([cum_row, factor_row, jnp.zeros((126, tokens), F32)], axis=0)
    )
    cum_col = turned[:, 0:1]
    factor_col = turned[:, 1:2]

    loads[2].wait()
    loads[3].wait()
    pl.semaphore_wait(barrier, len(known))

    tail = pl.ds(tokens - 16, 16)
    follower = seq_at((me + 1) % shards)
    halos = [
        remote(ref.at[tail, :], halo_recv.at[i], halo_sem.at[2 * i], halo_sem.at[2 * i + 1], follower)
        for i, ref in enumerate((k_ref, q_ref))
    ]
    halos[0].start()
    for step in (4, 3, 5, 2, 6, 1, 7):
        pl.semaphore_signal(
            rows_sem, inc=1, device_id=seq_at(y_peer(step)), device_id_type=MESH
        )
    for step in (4, 3, 5, 2, 6, 1, 7):
        remote(
            scal_ref.at[me], scal_ref.at[me], scal_sem.at[0], scal_sem.at[1], seq_at(z_peer(step))
        ).start()
    halos[1].start()

    def conv_silu(which, first, count):
        begin = begin_col[first : first + count]
        position = t_col[first : first + count]
        running = taps_ref[which, 0:1, :] * ext_ref[8 + first : 8 + first + count, :]
        for lag in range(1, taps_ref.shape[1]):
            keep = (position - lag) >= begin
            keep = jnp.concatenate([keep.astype(F32)] * (width // 128), axis=1) > 0.0
            shifted = ext_ref[8 + first - lag : 8 + first - lag + count, :]
            running = running + jnp.where(keep, taps_ref[which, lag : lag + 1, :] * shifted, 0.0)
        return (running / (1.0 + jnp.exp(-running))).astype(BF16)

    def outer_sum(left, right):
        return lax.dot_general(
            left, right, (((0,), (0,)), ((), ())), preferred_element_type=F32
        )

    loads[4].wait()
    loads[5].wait()
    ext_ref[8 : 8 + tokens, :] = k_ref[...].astype(F32)
    key_rest = conv_silu(1, 16, tokens - 16)
    weighted_rest = key_rest.astype(F32) * factor_col[16:]
    memory_rest = outer_sum(weighted_rest.astype(BF16), v_ref[16:, :])
    normal_rest = jnp.sum(weighted_rest, axis=0, keepdims=True)
    halos[0].wait_recv()
    ext_ref[0:8, :] = halo_recv[0, 8:16, :].astype(F32)
    key_first = conv_silu(1, 0, 16)
    weighted_first = key_first.astype(F32) * factor_col[:16]
    memory = (memory_rest + outer_sum(weighted_first.astype(BF16), v_ref[:16, :])).astype(BF16)
    key = jnp.concatenate([key_first, key_rest], axis=0)
    value = v_ref[...]
    tile_rows = width // 16
    for c in range(values // 128):
        own_tiles[c * tile_rows : (c + 1) * tile_rows] = memory[
            :, c * 128 : (c + 1) * 128
        ].reshape(tile_rows, 16, 128)
    normal = normal_rest + jnp.sum(weighted_first, axis=0, keepdims=True)
    norm_z[my_z] = jnp.concatenate([normal[:, 0:128], normal[:, 128:256]], axis=0)

    def far(step):
        dy, dz = step // SIDE, step % SIDE
        return -(min(dy, rows - dy) + min(dz, SIDE - dz))

    steps = sorted(range(1, shards), key=far)

    def peer_at(step):
        return ((my_y + step // SIDE) % rows) * SIDE + (my_z + step % SIDE) % SIDE

    def send_tiles(chosen):
        for step in chosen:
            peer = peer_at(step)
            remote(
                own_tiles.at[peer], got_tiles.at[me], tile_sem.at[0], tile_sem.at[1], seq_at(peer)
            ).start()

    pl.semaphore_wait(rows_sem, rows - 1)
    send_tiles(steps[:24])

    some = pl.ds(0, SIDE - 1)
    remote(
        scal_ref.at[some], scal_ref.at[some], scal_sem.at[0], scal_sem.at[1], seq_at(me)
    ).wait_recv()
    mine = pl.ds(my_y * SIDE, SIDE)
    for step in range(1, rows):
        remote(
            scal_ref.at[mine],
            scal_ref.at[mine],
            scal_sem.at[2],
            scal_sem.at[3],
            seq_at(y_peer(step)),
        ).start()
    send_tiles(steps[24:])
    for step in range(1, SIDE):
        remote(
            norm_z.at[my_z], norm_z.at[my_z], norm_sem.at[0], norm_sem.at[1], seq_at(z_peer(step))
        ).start()
    got_tiles[me] = own_tiles[me]

    halos[1].wait_recv()
    ext_ref[0:8, :] = halo_recv[1, 8:16, :].astype(F32)
    ext_ref[8 : 8 + tokens, :] = q_ref[...].astype(F32)
    query = conv_silu(0, 0, tokens)
    scores = (
        lax.dot_general(query, key, (((1,), (1,)), ((), ())), preferred_element_type=F32) * scale
    )

    most = pl.ds(0, (rows - 1) * SIDE)
    remote(
        scal_ref.at[most], scal_ref.at[most], scal_sem.at[2], scal_sem.at[3], seq_at(me)
    ).wait_recv()
    level = jnp.full((1, 128), NEG, F32)
    for s in range(shards):
        pair = scal_ref[s]
        stab_s, thr_s = pair[0:1, :], pair[1:2, :]
        m_rows[s : s + 1, :] = level
        carried_on = level + thr_s
        level = jnp.maximum(stab_s, carried_on)
        stab_rows[s : s + 1, :] = stab_s - level
        thr_rows[s : s + 1, :] = carried_on - level
    a_rows[...] = jnp.exp(thr_rows[...])
    b_rows[...] = jnp.exp(stab_rows[...])

    most_tiles = pl.ds(0, shards - 1)
    remote(
        got_tiles.at[most_tiles],
        got_tiles.at[most_tiles],
        tile_sem.at[0],
        tile_sem.at[1],
        seq_at(me),
    ).wait_recv()
    some_norm = pl.ds(0, SIDE - 1)
    remote(
        norm_z.at[some_norm], norm_z.at[some_norm], norm_sem.at[0], norm_sem.at[1], seq_at(me)
    ).wait_recv()
    total = jnp.zeros((2, 128), F32)
    for z in range(SIDE):
        at = pl.ds(my_y * SIDE + z, 1)
        total = a_rows[at, :] * total + b_rows[at, :] * norm_z[z]
    norm_y[my_y] = total
    for step in range(1, rows):
        remote(
            norm_y.at[my_y], norm_y.at[my_y], norm_sem.at[2], norm_sem.at[3], seq_at(y_peer(step))
        ).start()

    state = jnp.zeros((16, 128), F32)
    for s in range(shards):
        back_tiles[s] = state.astype(BF16)
        state = a_rows[s : s + 1, :] * state + b_rows[s : s + 1, :] * got_tiles[s].astype(F32)

    def send_back(peer):
        remote(
            back_tiles.at[peer], mem_tiles.at[me], tile_sem.at[2], tile_sem.at[3], seq_at(peer)
        ).start()

    for y in range(2):
        for z in range(2):
            pl.when((my_y != y) | (my_z != z))(functools.partial(send_back, y * SIDE + z))
    for step in steps:
        peer = peer_at(step)
        late = (peer // SIDE >= 2) | (peer % SIDE >= 2)
        pl.when(late)(functools.partial(send_back, peer))
    mem_tiles[me] = back_tiles[me]

    m_in = m_rows[pl.ds(me, 1), :][:, 0:1]
    begin_full = jnp.concatenate([begin_col] * (tokens // 128), axis=1)
    allowed = (s_full <= t_full) & (s_full >= begin_full)
    log_weight = jnp.where(allowed, gain_row + cum_col, NEG)
    carried = jnp.where(begin_col[:, 0:1] < 0, m_in + cum_col, NEG)
    row_max = jnp.maximum(jnp.max(log_weight, axis=1, keepdims=True), carried)
    weights = scores * jnp.exp(log_weight - row_max)
    reach = jnp.exp(carried - row_max) * scale
    num_ref[...] = jnp.dot(weights.astype(BF16), value, preferred_element_type=F32)
    den_inside = jnp.sum(weights, axis=1, keepdims=True)


    some_y = pl.ds(0, rows - 1)
    remote(
        norm_y.at[some_y], norm_y.at[some_y], norm_sem.at[2], norm_sem.at[3], seq_at(me)
    ).wait_recv()
    norm_in = jnp.zeros((2, 128), F32)
    for y in range(rows):
        decay = a_rows[y * SIDE : y * SIDE + 1, :]
        for z in range(1, SIDE):
            decay = decay * a_rows[y * SIDE + z : y * SIDE + z + 1, :]
        norm_in = jnp.where(y < my_y, decay * norm_in + norm_y[y], norm_in)
    for z in range(SIDE):
        at = pl.ds(my_y * SIDE + z, 1)
        norm_in = jnp.where(
            z < my_z, a_rows[at, :] * norm_in + b_rows[at, :] * norm_z[z], norm_in
        )
    norm_row = jnp.concatenate([norm_in[0:1, :], norm_in[1:2, :]], axis=1)
    from_normal = jnp.sum(query.astype(F32) * norm_row, axis=1, keepdims=True)
    floor = jnp.maximum(jnp.abs(den_inside + reach * from_normal), 1.0)
    inverse = 1.0 / floor

    loads[6].wait()
    remote(
        mem_tiles.at[most_tiles],
        mem_tiles.at[most_tiles],
        tile_sem.at[2],
        tile_sem.at[3],
        seq_at(me),
    ).wait_recv()
    parts = []
    for c in range(values // 128):
        block = mem_tiles[c * tile_rows : (c + 1) * tile_rows].reshape(width, 128)
        from_memory = jnp.dot(query, block, preferred_element_type=F32)
        at = slice(c * 128, (c + 1) * 128)
        parts.append(((num_ref[:, at] + reach * from_memory) * inverse).astype(BF16))
    head_out = jnp.concatenate(parts, axis=1)

    out_cols = out_ref.shape[1]
    half = tokens // 2

    def project(x, core):
        column = pl.multiple_of((2 * x + core) * out_cols, out_cols)
        return jnp.dot(head_out, wo_ref[:, pl.ds(column, out_cols)], preferred_element_type=F32)

    pair_copies = {}

    def pair_start(step):
        pair_send[step] = project((my_x + step) % chips, 1 - my_c).astype(BF16)
        pair_copies[step] = remote(
            pair_send.at[step],
            pair_recv.at[step],
            pair_ssem.at[step],
            pair_rsem.at[step],
            head_at(partner),
        )
        pair_copies[step].start()

    def chip_sum(step):
        ours = project((my_x + step) % chips, my_c)
        pair_copies[step].wait_recv()
        return ours + pair_recv[step].astype(F32)

    def x_copy(slot, where):
        return remote(
            x_send.at[slot], x_recv.at[slot], x_ssem.at[slot], x_rsem.at[slot], head_at(where)
        )

    x_copies = [x_copy(slot, x_next if slot % 2 == 0 else x_prev) for slot in range(6)]
    pair_start(2)
    pair_start(1)
    pair_start(3)
    pair_start(0)
    opposite = chip_sum(2)
    x_send[0] = opposite[:half].astype(BF16)
    x_copies[0].start()
    x_send[1] = opposite[half:].astype(BF16)
    x_copies[1].start()
    after = chip_sum(1)
    x_send[2] = after[half:].astype(BF16)
    x_copies[2].start()
    before = chip_sum(3)
    x_send[3] = before[:half].astype(BF16)
    x_copies[3].start()
    x_copies[0].wait_recv()
    x_send[4] = (after[:half] + x_recv[0].astype(F32)).astype(BF16)
    x_copies[4].start()
    x_copies[1].wait_recv()
    x_send[5] = (before[half:] + x_recv[1].astype(F32)).astype(BF16)
    x_copies[5].start()
    both = chip_sum(0)
    x_copies[3].wait_recv()
    x_copies[4].wait_recv()
    out_ref[:half] = (both[:half] + x_recv[3].astype(F32) + x_recv[4].astype(F32)).astype(BF16)
    x_copies[2].wait_recv()
    x_copies[5].wait_recv()
    out_ref[half:] = (both[half:] + x_recv[2].astype(F32) + x_recv[5].astype(F32)).astype(BF16)

    for copy in halos:
        copy.wait_send()
    remote(
        scal_ref.at[some], scal_ref.at[some], scal_sem.at[0], scal_sem.at[1], seq_at(me)
    ).wait_send()
    remote(
        scal_ref.at[most], scal_ref.at[most], scal_sem.at[2], scal_sem.at[3], seq_at(me)
    ).wait_send()
    remote(
        norm_z.at[some_norm], norm_z.at[some_norm], norm_sem.at[0], norm_sem.at[1], seq_at(me)
    ).wait_send()
    remote(
        norm_y.at[some_y], norm_y.at[some_y], norm_sem.at[2], norm_sem.at[3], seq_at(me)
    ).wait_send()
    for first, tiles in ((0, own_tiles), (2, back_tiles)):
        remote(
            tiles.at[most_tiles],
            tiles.at[most_tiles],
            tile_sem.at[first],
            tile_sem.at[first + 1],
            seq_at(me),
        ).wait_send()
    for copy in list(pair_copies.values()) + x_copies:
        copy.wait_send()


def on_device(
    shards,
    chips,
    query_input,
    key_input,
    value_input,
    kernel_taps,
    input_gate,
    forget_gate,
    request_lengths,
    output_weight,
):
    tokens, width = query_input.shape
    values = value_input.shape[1]
    out_cols = output_weight.shape[1] // (2 * chips)
    vmem = pl.BlockSpec(memory_space=pltpu.VMEM)
    dma = pltpu.SemaphoreType.DMA
    return pl.pallas_call(
        functools.partial(kernel, shards, chips),
        out_shape=jax.ShapeDtypeStruct((tokens, out_cols), BF16),
        in_specs=[pl.BlockSpec(memory_space=pltpu.HBM)] * 8,
        out_specs=vmem,
        scratch_shapes=[pltpu.SMEM(request_lengths.shape, jnp.int32)]
        + [
            pltpu.VMEM(a.shape, a.dtype)
            for a in (
                query_input,
                key_input,
                value_input,
                kernel_taps,
                input_gate,
                forget_gate,
            )
        ]
        + [
            pltpu.VMEM(output_weight.shape, BF16),
            pltpu.VMEM((tokens + 8, width), F32),
            pltpu.VMEM((2, 16, width), BF16),
            pltpu.VMEM((shards, 2, 128), F32),
            pltpu.VMEM((shards, 128), F32),
            pltpu.VMEM((shards, 128), F32),
            pltpu.VMEM((shards, 128), F32),
            pltpu.VMEM((shards, 128), F32),
            pltpu.VMEM((shards, 128), F32),
            pltpu.VMEM((shards, 16, 128), BF16),
            pltpu.VMEM((shards, 16, 128), BF16),
            pltpu.VMEM((shards, 16, 128), BF16),
            pltpu.VMEM((shards, 16, 128), BF16),
            pltpu.VMEM((SIDE, 2, 128), F32),
            pltpu.VMEM((shards // SIDE, 2, 128), F32),
            pltpu.VMEM((tokens, values), F32),
            pltpu.VMEM((chips, tokens, out_cols), BF16),
            pltpu.VMEM((chips, tokens, out_cols), BF16),
            pltpu.VMEM((6, tokens // 2, out_cols), BF16),
            pltpu.VMEM((6, tokens // 2, out_cols), BF16),
            dma((8,)),
            dma((4,)),
            dma((4,)),
            dma((4,)),
            dma((4,)),
            dma((chips,)),
            dma((chips,)),
            dma((6,)),
            dma((6,)),
            pltpu.SemaphoreType.REGULAR,
        ],
        compiler_params=pltpu.CompilerParams(
            collective_id=0, has_side_effects=True, vmem_limit_bytes=32 << 20
        ),
    )(
        *(
            pltpu.with_memory_space_constraint(a, pltpu.HBM)
            for a in (
                request_lengths,
                query_input,
                key_input,
                value_input,
                kernel_taps,
                input_gate,
                forget_gate,
                output_weight,
            )
        ),
    )


def solution(mesh):
    placed = (
        P("seq", "head"),
        P("seq", "head"),
        P("seq", "head"),
        P(None, None, "head"),
        P("head", "seq"),
        P("head", "seq"),
        P(),
        P("head", None),
    )
    return jax.shard_map(
        functools.partial(on_device, mesh.shape["seq"], mesh.shape["head"] // 2),
        mesh=mesh,
        in_specs=placed,
        out_specs=P("seq", "head"),
        check_vma=False,
    )
```

```python
import functools

import jax
import jax.numpy as jnp
from jax import lax
from jax.experimental import pallas as pl
from jax.experimental.pallas import tpu as pltpu
from jax.sharding import PartitionSpec as P

MESH = pl.DeviceIdType.MESH
NEG = -1e30
SIDE = 8
F32 = jnp.float32
BF16 = jnp.bfloat16


def kernel(
    shards,
    chips,
    len_hbm,
    q_hbm,
    k_hbm,
    v_hbm,
    taps_hbm,
    ig_hbm,
    fg_hbm,
    wo_hbm,
    out_ref,
    len_ref,
    q_ref,
    k_ref,
    v_ref,
    taps_ref,
    ig_ref,
    fg_ref,
    wo_ref,
    ext_ref,
    halo_recv,
    scal_ref,
    stab_rows,
    thr_rows,
    m_rows,
    a_rows,
    b_rows,
    own_tiles,
    got_tiles,
    back_tiles,
    mem_tiles,
    norm_z,
    norm_y,
    num_ref,
    pair_send,
    pair_recv,
    x_send,
    x_recv,
    load_sem,
    halo_sem,
    scal_sem,
    norm_sem,
    tile_sem,
    pair_ssem,
    pair_rsem,
    x_ssem,
    x_rsem,
    rows_sem,
):
    tokens, width = q_hbm.shape
    values = v_hbm.shape[1]
    scale = 1.0 / (width**0.5)
    me = lax.axis_index("seq")
    head = lax.axis_index("head")
    my_y, my_z = me // SIDE, me % SIDE
    my_x, my_c = head // 2, head % 2
    rows = shards // SIDE

    def seq_at(index):
        return {"seq": index}

    def head_at(index):
        return {"head": index}

    def remote(src, dst, ssem, rsem, where):
        return pltpu.make_async_remote_copy(
            src_ref=src, dst_ref=dst, send_sem=ssem, recv_sem=rsem, device_id=where, device_id_type=MESH
        )

    barrier = pltpu.get_barrier_semaphore()

    def z_peer(step):
        return my_y * SIDE + (my_z + step) % SIDE

    def y_peer(step):
        return ((my_y + step) % rows) * SIDE + my_z

    partner = 2 * my_x + (1 - my_c)
    x_next = 2 * ((my_x + 1) % chips) + my_c
    x_prev = 2 * ((my_x + chips - 1) % chips) + my_c
    known = [seq_at((me + shards - 1) % shards)]
    known += [seq_at(z_peer(step)) for step in (4, 3, 5, 2, 6, 1, 7)]
    known += [seq_at(y_peer(step)) for step in (4, 3, 5, 2, 6, 1, 7)]
    known += [head_at(partner), head_at(x_next), head_at(x_prev)]
    for where in known:
        pl.semaphore_signal(barrier, inc=1, device_id=where, device_id_type=MESH)

    loads = [
        pltpu.make_async_copy(src, dst, load_sem.at[i])
        for i, (src, dst) in enumerate(
            (
                (fg_hbm, fg_ref),
                (ig_hbm, ig_ref),
                (k_hbm, k_ref),
                (q_hbm, q_ref),
                (taps_hbm, taps_ref),
                (v_hbm, v_ref),
                (wo_hbm, wo_ref),
                (len_hbm, len_ref),
            )
        )
    ]
    for load in loads:
        load.start()

    loads[7].wait()
    offset = me * tokens
    starts = [jnp.int32(0)]
    for r in range(len_ref.shape[0] - 1):
        starts.append(starts[-1] + len_ref[r])

    def request_start(position):
        found = jnp.zeros_like(position)
        for start in starts[1:]:
            found = jnp.where(start <= position, start, found)
        return found

    t_col = lax.broadcasted_iota(jnp.int32, (tokens, 128), 0)
    begin_col = request_start(t_col + offset) - offset
    s_row = lax.broadcasted_iota(jnp.int32, (1, tokens), 1)
    last_begin = jnp.int32(0)
    for start in starts[1:]:
        last_begin = jnp.where(start <= offset + (tokens - 1), start, last_begin)
    last_begin = last_begin - offset

    loads[0].wait()
    loads[1].wait()
    fg = fg_ref[...]
    ig = ig_ref[...]
    log_forget = -(jnp.maximum(-fg, 0.0) + jnp.log1p(jnp.exp(-jnp.abs(fg))))
    hi = log_forget.astype(BF16)
    rest = log_forget - hi.astype(F32)
    mid = rest.astype(BF16)
    low = (rest - mid.astype(F32)).astype(BF16)
    pieces = jnp.concatenate(
        [hi.astype(F32), mid.astype(F32), low.astype(F32), jnp.zeros((5, tokens), F32)], axis=0
    ).astype(BF16)
    t_full = lax.broadcasted_iota(jnp.int32, (tokens, tokens), 0)
    s_full = lax.broadcasted_iota(jnp.int32, (tokens, tokens), 1)
    upper = jnp.where(t_full <= s_full, 1.0, 0.0).astype(BF16)
    cum_row = jnp.sum(
        jnp.dot(pieces, upper, preferred_element_type=F32), axis=0, keepdims=True
    )
    cum_last = cum_row[:, tokens - 1 : tokens]
    gain_row = ig - cum_row
    tail_row = jnp.where(s_row >= last_begin, gain_row + cum_last, NEG)
    stab = jnp.max(tail_row, axis=1, keepdims=True)
    factor_row = jnp.exp(tail_row - stab)
    through = jnp.where(last_begin < 0, cum_last, NEG)
    scal_ref[me] = jnp.concatenate(
        [jnp.broadcast_to(stab, (1, 128)), jnp.broadcast_to(through, (1, 128))], axis=0
    )
    turned = jnp.transpose(
        jnp.concatenate([cum_row, factor_row, jnp.zeros((126, tokens), F32)], axis=0)
    )
    cum_col = turned[:, 0:1]
    factor_col = turned[:, 1:2]

    loads[2].wait()
    loads[3].wait()
    pl.semaphore_wait(barrier, len(known))

    tail = pl.ds(tokens - 16, 16)
    follower = seq_at((me + 1) % shards)
    halos = [
        remote(ref.at[tail, :], halo_recv.at[i], halo_sem.at[2 * i], halo_sem.at[2 * i + 1], follower)
        for i, ref in enumerate((k_ref, q_ref))
    ]
    halos[0].start()
    for step in (4, 3, 5, 2, 6, 1, 7):
        pl.semaphore_signal(
            rows_sem, inc=1, device_id=seq_at(y_peer(step)), device_id_type=MESH
        )
    for step in (4, 3, 5, 2, 6, 1, 7):
        remote(
            scal_ref.at[me], scal_ref.at[me], scal_sem.at[0], scal_sem.at[1], seq_at(z_peer(step))
        ).start()
    halos[1].start()

    def conv_silu(which, first, count):
        begin = begin_col[first : first + count]
        position = t_col[first : first + count]
        running = taps_ref[which, 0:1, :] * ext_ref[8 + first : 8 + first + count, :]
        for lag in range(1, taps_ref.shape[1]):
            keep = (position - lag) >= begin
            keep = jnp.concatenate([keep.astype(F32)] * (width // 128), axis=1) > 0.0
            shifted = ext_ref[8 + first - lag : 8 + first - lag + count, :]
            running = running + jnp.where(keep, taps_ref[which, lag : lag + 1, :] * shifted, 0.0)
        return (running / (1.0 + jnp.exp(-running))).astype(BF16)

    def outer_sum(left, right):
        return lax.dot_general(
            left, right, (((0,), (0,)), ((), ())), preferred_element_type=F32
        )

    loads[4].wait()
    loads[5].wait()
    ext_ref[8 : 8 + tokens, :] = k_ref[...].astype(F32)
    key_rest = conv_silu(1, 16, tokens - 16)
    weighted_rest = key_rest.astype(F32) * factor_col[16:]
    memory_rest = outer_sum(weighted_rest.astype(BF16), v_ref[16:, :])
    normal_rest = jnp.sum(weighted_rest, axis=0, keepdims=True)
    halos[0].wait_recv()
    ext_ref[0:8, :] = halo_recv[0, 8:16, :].astype(F32)
    key_first = conv_silu(1, 0, 16)
    weighted_first = key_first.astype(F32) * factor_col[:16]
    memory = (memory_rest + outer_sum(weighted_first.astype(BF16), v_ref[:16, :])).astype(BF16)
    key = jnp.concatenate([key_first, key_rest], axis=0)
    value = v_ref[...]
    tile_rows = width // 16
    for c in range(values // 128):
        own_tiles[c * tile_rows : (c + 1) * tile_rows] = memory[
            :, c * 128 : (c + 1) * 128
        ].reshape(tile_rows, 16, 128)
    normal = normal_rest + jnp.sum(weighted_first, axis=0, keepdims=True)
    norm_z[my_z] = jnp.concatenate([normal[:, 0:128], normal[:, 128:256]], axis=0)

    def far(step):
        dy, dz = step // SIDE, step % SIDE
        return -(min(dy, rows - dy) + min(dz, SIDE - dz))

    steps = sorted(range(1, shards), key=far)

    def peer_at(step):
        return ((my_y + step // SIDE) % rows) * SIDE + (my_z + step % SIDE) % SIDE

    def send_tiles(chosen):
        for step in chosen:
            peer = peer_at(step)
            remote(
                own_tiles.at[peer], got_tiles.at[me], tile_sem.at[0], tile_sem.at[1], seq_at(peer)
            ).start()

    pl.semaphore_wait(rows_sem, rows - 1)
    send_tiles(steps[:24])

    some = pl.ds(0, SIDE - 1)
    remote(
        scal_ref.at[some], scal_ref.at[some], scal_sem.at[0], scal_sem.at[1], seq_at(me)
    ).wait_recv()
    mine = pl.ds(my_y * SIDE, SIDE)
    for step in range(1, rows):
        remote(
            scal_ref.at[mine],
            scal_ref.at[mine],
            scal_sem.at[2],
            scal_sem.at[3],
            seq_at(y_peer(step)),
        ).start()
    send_tiles(steps[24:])
    for step in range(1, SIDE):
        remote(
            norm_z.at[my_z], norm_z.at[my_z], norm_sem.at[0], norm_sem.at[1], seq_at(z_peer(step))
        ).start()
    got_tiles[me] = own_tiles[me]

    halos[1].wait_recv()
    ext_ref[0:8, :] = halo_recv[1, 8:16, :].astype(F32)
    ext_ref[8 : 8 + tokens, :] = q_ref[...].astype(F32)
    query = conv_silu(0, 0, tokens)
    scores = (
        lax.dot_general(query, key, (((1,), (1,)), ((), ())), preferred_element_type=F32) * scale
    )

    most = pl.ds(0, (rows - 1) * SIDE)
    remote(
        scal_ref.at[most], scal_ref.at[most], scal_sem.at[2], scal_sem.at[3], seq_at(me)
    ).wait_recv()
    level = jnp.full((1, 128), NEG, F32)
    for s in range(shards):
        pair = scal_ref[s]
        stab_s, thr_s = pair[0:1, :], pair[1:2, :]
        m_rows[s : s + 1, :] = level
        carried_on = level + thr_s
        level = jnp.maximum(stab_s, carried_on)
        stab_rows[s : s + 1, :] = stab_s - level
        thr_rows[s : s + 1, :] = carried_on - level
    a_rows[...] = jnp.exp(thr_rows[...])
    b_rows[...] = jnp.exp(stab_rows[...])

    most_tiles = pl.ds(0, shards - 1)
    remote(
        got_tiles.at[most_tiles],
        got_tiles.at[most_tiles],
        tile_sem.at[0],
        tile_sem.at[1],
        seq_at(me),
    ).wait_recv()
    some_norm = pl.ds(0, SIDE - 1)
    remote(
        norm_z.at[some_norm], norm_z.at[some_norm], norm_sem.at[0], norm_sem.at[1], seq_at(me)
    ).wait_recv()
    total = jnp.zeros((2, 128), F32)
    for z in range(SIDE):
        at = pl.ds(my_y * SIDE + z, 1)
        total = a_rows[at, :] * total + b_rows[at, :] * norm_z[z]
    norm_y[my_y] = total
    for step in range(1, rows):
        remote(
            norm_y.at[my_y], norm_y.at[my_y], norm_sem.at[2], norm_sem.at[3], seq_at(y_peer(step))
        ).start()

    state = jnp.zeros((16, 128), F32)
    for s in range(shards):
        back_tiles[s] = state.astype(BF16)
        state = a_rows[s : s + 1, :] * state + b_rows[s : s + 1, :] * got_tiles[s].astype(F32)

    def send_back(peer):
        remote(
            back_tiles.at[peer], mem_tiles.at[me], tile_sem.at[2], tile_sem.at[3], seq_at(peer)
        ).start()

    def to_first(step):
        peer = ((my_y + step) % rows) * SIDE
        pl.when((peer != 0) & (peer != me))(functools.partial(send_back, peer))

    def to_other(step):
        peer = peer_at(step)
        pl.when(peer % SIDE != 0)(functools.partial(send_back, peer))

    for step in (4, 3, 5, 2, 6, 1, 7, 0):
        to_first(step)
    for step in steps:
        to_other(step)

    @pl.when(me == 0)
    def _():
        mem_tiles[...] = jnp.zeros(mem_tiles.shape, BF16)

    @pl.when(me != 0)
    def _():
        mem_tiles[me] = back_tiles[me]


    m_in = m_rows[pl.ds(me, 1), :][:, 0:1]
    begin_full = jnp.concatenate([begin_col] * (tokens // 128), axis=1)
    allowed = (s_full <= t_full) & (s_full >= begin_full)
    log_weight = jnp.where(allowed, gain_row + cum_col, NEG)
    carried = jnp.where(begin_col[:, 0:1] < 0, m_in + cum_col, NEG)
    row_max = jnp.maximum(jnp.max(log_weight, axis=1, keepdims=True), carried)
    weights = scores * jnp.exp(log_weight - row_max)
    reach = jnp.exp(carried - row_max) * scale
    num_ref[...] = jnp.dot(weights.astype(BF16), value, preferred_element_type=F32)
    den_inside = jnp.sum(weights, axis=1, keepdims=True)


    some_y = pl.ds(0, rows - 1)
    remote(
        norm_y.at[some_y], norm_y.at[some_y], norm_sem.at[2], norm_sem.at[3], seq_at(me)
    ).wait_recv()
    norm_in = jnp.zeros((2, 128), F32)
    for y in range(rows):
        decay = a_rows[y * SIDE : y * SIDE + 1, :]
        for z in range(1, SIDE):
            decay = decay * a_rows[y * SIDE + z : y * SIDE + z + 1, :]
        norm_in = jnp.where(y < my_y, decay * norm_in + norm_y[y], norm_in)
    for z in range(SIDE):
        at = pl.ds(my_y * SIDE + z, 1)
        norm_in = jnp.where(
            z < my_z, a_rows[at, :] * norm_in + b_rows[at, :] * norm_z[z], norm_in
        )
    norm_row = jnp.concatenate([norm_in[0:1, :], norm_in[1:2, :]], axis=1)
    from_normal = jnp.sum(query.astype(F32) * norm_row, axis=1, keepdims=True)
    floor = jnp.maximum(jnp.abs(den_inside + reach * from_normal), 1.0)
    inverse = 1.0 / floor

    loads[6].wait()
    @pl.when(me != 0)
    def _():
        remote(
            mem_tiles.at[most_tiles],
            mem_tiles.at[most_tiles],
            tile_sem.at[2],
            tile_sem.at[3],
            seq_at(me),
        ).wait_recv()

    parts = []
    for c in range(values // 128):
        block = mem_tiles[c * tile_rows : (c + 1) * tile_rows].reshape(width, 128)
        from_memory = jnp.dot(query, block, preferred_element_type=F32)
        at = slice(c * 128, (c + 1) * 128)
        parts.append(((num_ref[:, at] + reach * from_memory) * inverse).astype(BF16))
    head_out = jnp.concatenate(parts, axis=1)

    out_cols = out_ref.shape[1]
    half = tokens // 2

    def project(x, core):
        column = pl.multiple_of((2 * x + core) * out_cols, out_cols)
        return jnp.dot(head_out, wo_ref[:, pl.ds(column, out_cols)], preferred_element_type=F32)

    pair_copies = {}

    def pair_start(step):
        pair_send[step] = project((my_x + step) % chips, 1 - my_c).astype(BF16)
        pair_copies[step] = remote(
            pair_send.at[step],
            pair_recv.at[step],
            pair_ssem.at[step],
            pair_rsem.at[step],
            head_at(partner),
        )
        pair_copies[step].start()

    def chip_sum(step):
        ours = project((my_x + step) % chips, my_c)
        pair_copies[step].wait_recv()
        return ours + pair_recv[step].astype(F32)

    def x_copy(slot, where):
        return remote(
            x_send.at[slot], x_recv.at[slot], x_ssem.at[slot], x_rsem.at[slot], head_at(where)
        )

    x_copies = [x_copy(slot, x_next if slot % 2 == 0 else x_prev) for slot in range(6)]
    pair_start(2)
    pair_start(1)
    pair_start(3)
    pair_start(0)
    opposite = chip_sum(2)
    x_send[0] = opposite[:half].astype(BF16)
    x_copies[0].start()
    x_send[1] = opposite[half:].astype(BF16)
    x_copies[1].start()
    after = chip_sum(1)
    x_send[2] = after[half:].astype(BF16)
    x_copies[2].start()
    before = chip_sum(3)
    x_send[3] = before[:half].astype(BF16)
    x_copies[3].start()
    x_copies[0].wait_recv()
    x_send[4] = (after[:half] + x_recv[0].astype(F32)).astype(BF16)
    x_copies[4].start()
    x_copies[1].wait_recv()
    x_send[5] = (before[half:] + x_recv[1].astype(F32)).astype(BF16)
    x_copies[5].start()
    both = chip_sum(0)
    x_copies[3].wait_recv()
    x_copies[4].wait_recv()
    out_ref[:half] = (both[:half] + x_recv[3].astype(F32) + x_recv[4].astype(F32)).astype(BF16)
    x_copies[2].wait_recv()
    x_copies[5].wait_recv()
    out_ref[half:] = (both[half:] + x_recv[2].astype(F32) + x_recv[5].astype(F32)).astype(BF16)

    for copy in halos:
        copy.wait_send()
    remote(
        scal_ref.at[some], scal_ref.at[some], scal_sem.at[0], scal_sem.at[1], seq_at(me)
    ).wait_send()
    remote(
        scal_ref.at[most], scal_ref.at[most], scal_sem.at[2], scal_sem.at[3], seq_at(me)
    ).wait_send()
    remote(
        norm_z.at[some_norm], norm_z.at[some_norm], norm_sem.at[0], norm_sem.at[1], seq_at(me)
    ).wait_send()
    remote(
        norm_y.at[some_y], norm_y.at[some_y], norm_sem.at[2], norm_sem.at[3], seq_at(me)
    ).wait_send()
    remote(
        own_tiles.at[most_tiles], own_tiles.at[most_tiles], tile_sem.at[0], tile_sem.at[1], seq_at(me)
    ).wait_send()
    back_sent = pl.ds(0, shards - 2)
    remote(
        back_tiles.at[back_sent], back_tiles.at[back_sent], tile_sem.at[2], tile_sem.at[3], seq_at(me)
    ).wait_send()

    @pl.when(me == 0)
    def _():
        remote(
            back_tiles.at[0], back_tiles.at[0], tile_sem.at[2], tile_sem.at[3], seq_at(me)
        ).wait_send()

    for copy in list(pair_copies.values()) + x_copies:
        copy.wait_send()


def on_device(
    shards,
    chips,
    query_input,
    key_input,
    value_input,
    kernel_taps,
    input_gate,
    forget_gate,
    request_lengths,
    output_weight,
):
    tokens, width = query_input.shape
    values = value_input.shape[1]
    out_cols = output_weight.shape[1] // (2 * chips)
    vmem = pl.BlockSpec(memory_space=pltpu.VMEM)
    dma = pltpu.SemaphoreType.DMA
    return pl.pallas_call(
        functools.partial(kernel, shards, chips),
        out_shape=jax.ShapeDtypeStruct((tokens, out_cols), BF16),
        in_specs=[pl.BlockSpec(memory_space=pltpu.HBM)] * 8,
        out_specs=vmem,
        scratch_shapes=[pltpu.SMEM(request_lengths.shape, jnp.int32)]
        + [
            pltpu.VMEM(a.shape, a.dtype)
            for a in (
                query_input,
                key_input,
                value_input,
                kernel_taps,
                input_gate,
                forget_gate,
            )
        ]
        + [
            pltpu.VMEM(output_weight.shape, BF16),
            pltpu.VMEM((tokens + 8, width), F32),
            pltpu.VMEM((2, 16, width), BF16),
            pltpu.VMEM((shards, 2, 128), F32),
            pltpu.VMEM((shards, 128), F32),
            pltpu.VMEM((shards, 128), F32),
            pltpu.VMEM((shards, 128), F32),
            pltpu.VMEM((shards, 128), F32),
            pltpu.VMEM((shards, 128), F32),
            pltpu.VMEM((shards, 16, 128), BF16),
            pltpu.VMEM((shards, 16, 128), BF16),
            pltpu.VMEM((shards, 16, 128), BF16),
            pltpu.VMEM((shards, 16, 128), BF16),
            pltpu.VMEM((SIDE, 2, 128), F32),
            pltpu.VMEM((shards // SIDE, 2, 128), F32),
            pltpu.VMEM((tokens, values), F32),
            pltpu.VMEM((chips, tokens, out_cols), BF16),
            pltpu.VMEM((chips, tokens, out_cols), BF16),
            pltpu.VMEM((6, tokens // 2, out_cols), BF16),
            pltpu.VMEM((6, tokens // 2, out_cols), BF16),
            dma((8,)),
            dma((4,)),
            dma((4,)),
            dma((4,)),
            dma((4,)),
            dma((chips,)),
            dma((chips,)),
            dma((6,)),
            dma((6,)),
            pltpu.SemaphoreType.REGULAR,
        ],
        compiler_params=pltpu.CompilerParams(
            collective_id=0, has_side_effects=True, vmem_limit_bytes=32 << 20
        ),
    )(
        *(
            pltpu.with_memory_space_constraint(a, pltpu.HBM)
            for a in (
                request_lengths,
                query_input,
                key_input,
                value_input,
                kernel_taps,
                input_gate,
                forget_gate,
                output_weight,
            )
        ),
    )


def solution(mesh):
    placed = (
        P("seq", "head"),
        P("seq", "head"),
        P("seq", "head"),
        P(None, None, "head"),
        P("head", "seq"),
        P("head", "seq"),
        P(),
        P("head", None),
    )
    return jax.shard_map(
        functools.partial(on_device, mesh.shape["seq"], mesh.shape["head"] // 2),
        mesh=mesh,
        in_specs=placed,
        out_specs=P("seq", "head"),
        check_vma=False,
    )
```

```python
import functools

import jax
import jax.numpy as jnp
from jax import lax
from jax.experimental import pallas as pl
from jax.experimental.pallas import tpu as pltpu
from jax.sharding import PartitionSpec as P

MESH = pl.DeviceIdType.MESH
NEG = -1e30
SIDE = 8
F32 = jnp.float32
BF16 = jnp.bfloat16


def kernel(
    shards,
    chips,
    len_hbm,
    q_hbm,
    k_hbm,
    v_hbm,
    taps_hbm,
    ig_hbm,
    fg_hbm,
    wo_hbm,
    out_ref,
    len_ref,
    q_ref,
    k_ref,
    v_ref,
    taps_ref,
    ig_ref,
    fg_ref,
    wo_ref,
    ext_ref,
    halo_recv,
    scal_ref,
    stab_rows,
    thr_rows,
    m_rows,
    a_rows,
    b_rows,
    own_tiles,
    got_tiles,
    back_tiles,
    mem_tiles,
    norm_z,
    norm_y,
    num_ref,
    pair_send,
    pair_recv,
    x_send,
    x_recv,
    load_sem,
    halo_sem,
    scal_sem,
    norm_sem,
    tile_sem,
    pair_ssem,
    pair_rsem,
    x_ssem,
    x_rsem,
    rows_sem,
):
    tokens, width = q_hbm.shape
    values = v_hbm.shape[1]
    scale = 1.0 / (width**0.5)
    me = lax.axis_index("seq")
    head = lax.axis_index("head")
    my_y, my_z = me // SIDE, me % SIDE
    my_x, my_c = head // 2, head % 2
    rows = shards // SIDE

    def seq_at(index):
        return {"seq": index}

    def head_at(index):
        return {"head": index}

    def remote(src, dst, ssem, rsem, where):
        return pltpu.make_async_remote_copy(
            src_ref=src, dst_ref=dst, send_sem=ssem, recv_sem=rsem, device_id=where, device_id_type=MESH
        )

    barrier = pltpu.get_barrier_semaphore()

    def z_peer(step):
        return my_y * SIDE + (my_z + step) % SIDE

    def y_peer(step):
        return ((my_y + step) % rows) * SIDE + my_z

    partner = 2 * my_x + (1 - my_c)
    x_next = 2 * ((my_x + 1) % chips) + my_c
    x_prev = 2 * ((my_x + chips - 1) % chips) + my_c
    known = [seq_at((me + shards - 1) % shards)]
    known += [seq_at(z_peer(step)) for step in (4, 3, 5, 2, 6, 1, 7)]
    known += [seq_at(y_peer(step)) for step in (4, 3, 5, 2, 6, 1, 7)]
    known += [head_at(partner), head_at(x_next), head_at(x_prev)]
    for where in known:
        pl.semaphore_signal(barrier, inc=1, device_id=where, device_id_type=MESH)

    loads = [
        pltpu.make_async_copy(src, dst, load_sem.at[i])
        for i, (src, dst) in enumerate(
            (
                (fg_hbm, fg_ref),
                (ig_hbm, ig_ref),
                (k_hbm, k_ref),
                (q_hbm, q_ref),
                (taps_hbm, taps_ref),
                (v_hbm, v_ref),
                (wo_hbm, wo_ref),
                (len_hbm, len_ref),
            )
        )
    ]
    for load in loads:
        load.start()

    loads[7].wait()
    offset = me * tokens
    starts = [jnp.int32(0)]
    for r in range(len_ref.shape[0] - 1):
        starts.append(starts[-1] + len_ref[r])

    def request_start(position):
        found = jnp.zeros_like(position)
        for start in starts[1:]:
            found = jnp.where(start <= position, start, found)
        return found

    t_col = lax.broadcasted_iota(jnp.int32, (tokens, 128), 0)
    begin_col = request_start(t_col + offset) - offset
    s_row = lax.broadcasted_iota(jnp.int32, (1, tokens), 1)
    last_begin = jnp.int32(0)
    for start in starts[1:]:
        last_begin = jnp.where(start <= offset + (tokens - 1), start, last_begin)
    last_begin = last_begin - offset

    loads[0].wait()
    loads[1].wait()
    fg = fg_ref[...]
    ig = ig_ref[...]
    log_forget = -(jnp.maximum(-fg, 0.0) + jnp.log1p(jnp.exp(-jnp.abs(fg))))
    hi = log_forget.astype(BF16)
    rest = log_forget - hi.astype(F32)
    mid = rest.astype(BF16)
    low = (rest - mid.astype(F32)).astype(BF16)
    pieces = jnp.concatenate(
        [hi.astype(F32), mid.astype(F32), low.astype(F32), jnp.zeros((5, tokens), F32)], axis=0
    ).astype(BF16)
    t_full = lax.broadcasted_iota(jnp.int32, (tokens, tokens), 0)
    s_full = lax.broadcasted_iota(jnp.int32, (tokens, tokens), 1)
    upper = jnp.where(t_full <= s_full, 1.0, 0.0).astype(BF16)
    cum_row = jnp.sum(
        jnp.dot(pieces, upper, preferred_element_type=F32), axis=0, keepdims=True
    )
    cum_last = cum_row[:, tokens - 1 : tokens]
    gain_row = ig - cum_row
    tail_row = jnp.where(s_row >= last_begin, gain_row + cum_last, NEG)
    stab = jnp.max(tail_row, axis=1, keepdims=True)
    factor_row = jnp.exp(tail_row - stab)
    through = jnp.where(last_begin < 0, cum_last, NEG)
    scal_ref[me] = jnp.concatenate(
        [jnp.broadcast_to(stab, (1, 128)), jnp.broadcast_to(through, (1, 128))], axis=0
    )
    turned = jnp.transpose(
        jnp.concatenate([cum_row, factor_row, jnp.zeros((126, tokens), F32)], axis=0)
    )
    cum_col = turned[:, 0:1]
    factor_col = turned[:, 1:2]

    loads[2].wait()
    loads[3].wait()
    pl.semaphore_wait(barrier, len(known))

    tail = pl.ds(tokens - 16, 16)
    follower = seq_at((me + 1) % shards)
    halos = [
        remote(ref.at[tail, :], halo_recv.at[i], halo_sem.at[2 * i], halo_sem.at[2 * i + 1], follower)
        for i, ref in enumerate((k_ref, q_ref))
    ]
    halos[0].start()
    for step in (4, 3, 5, 2, 6, 1, 7):
        pl.semaphore_signal(
            rows_sem, inc=1, device_id=seq_at(y_peer(step)), device_id_type=MESH
        )
    for step in (4, 3, 5, 2, 6, 1, 7):
        remote(
            scal_ref.at[me], scal_ref.at[me], scal_sem.at[0], scal_sem.at[1], seq_at(z_peer(step))
        ).start()
    halos[1].start()

    def conv_silu(which, first, count):
        begin = begin_col[first : first + count]
        position = t_col[first : first + count]
        running = taps_ref[which, 0:1, :] * ext_ref[8 + first : 8 + first + count, :]
        for lag in range(1, taps_ref.shape[1]):
            keep = (position - lag) >= begin
            keep = jnp.concatenate([keep.astype(F32)] * (width // 128), axis=1) > 0.0
            shifted = ext_ref[8 + first - lag : 8 + first - lag + count, :]
            running = running + jnp.where(keep, taps_ref[which, lag : lag + 1, :] * shifted, 0.0)
        return (running / (1.0 + jnp.exp(-running))).astype(BF16)

    def outer_sum(left, right):
        return lax.dot_general(
            left, right, (((0,), (0,)), ((), ())), preferred_element_type=F32
        )

    loads[4].wait()
    loads[5].wait()
    ext_ref[8 : 8 + tokens, :] = k_ref[...].astype(F32)
    key_rest = conv_silu(1, 16, tokens - 16)
    weighted_rest = key_rest.astype(F32) * factor_col[16:]
    memory_rest = outer_sum(weighted_rest.astype(BF16), v_ref[16:, :])
    normal_rest = jnp.sum(weighted_rest, axis=0, keepdims=True)
    halos[0].wait_recv()
    ext_ref[0:8, :] = halo_recv[0, 8:16, :].astype(F32)
    key_first = conv_silu(1, 0, 16)
    weighted_first = key_first.astype(F32) * factor_col[:16]
    memory = (memory_rest + outer_sum(weighted_first.astype(BF16), v_ref[:16, :])).astype(BF16)
    key = jnp.concatenate([key_first, key_rest], axis=0)
    value = v_ref[...]
    tile_rows = width // 16
    for c in range(values // 128):
        own_tiles[c * tile_rows : (c + 1) * tile_rows] = memory[
            :, c * 128 : (c + 1) * 128
        ].reshape(tile_rows, 16, 128)
    normal = normal_rest + jnp.sum(weighted_first, axis=0, keepdims=True)
    norm_z[my_z] = jnp.concatenate([normal[:, 0:128], normal[:, 128:256]], axis=0)

    def far(step):
        dy, dz = step // SIDE, step % SIDE
        return -(min(dy, rows - dy) + min(dz, SIDE - dz))

    steps = sorted(range(1, shards), key=far)

    def peer_at(step):
        return ((my_y + step // SIDE) % rows) * SIDE + (my_z + step % SIDE) % SIDE

    def send_tiles(chosen):
        for step in chosen:
            peer = peer_at(step)
            remote(
                own_tiles.at[peer], got_tiles.at[me], tile_sem.at[0], tile_sem.at[1], seq_at(peer)
            ).start()

    pl.semaphore_wait(rows_sem, rows - 1)
    send_tiles(steps[:24])

    some = pl.ds(0, SIDE - 1)
    remote(
        scal_ref.at[some], scal_ref.at[some], scal_sem.at[0], scal_sem.at[1], seq_at(me)
    ).wait_recv()
    mine = pl.ds(my_y * SIDE, SIDE)
    for step in range(1, rows):
        remote(
            scal_ref.at[mine],
            scal_ref.at[mine],
            scal_sem.at[2],
            scal_sem.at[3],
            seq_at(y_peer(step)),
        ).start()
    send_tiles(steps[24:])
    for step in range(1, SIDE):
        remote(
            norm_z.at[my_z], norm_z.at[my_z], norm_sem.at[0], norm_sem.at[1], seq_at(z_peer(step))
        ).start()
    got_tiles[me] = own_tiles[me]

    halos[1].wait_recv()
    ext_ref[0:8, :] = halo_recv[1, 8:16, :].astype(F32)
    ext_ref[8 : 8 + tokens, :] = q_ref[...].astype(F32)
    query = conv_silu(0, 0, tokens)
    scores = (
        lax.dot_general(query, key, (((1,), (1,)), ((), ())), preferred_element_type=F32) * scale
    )

    most = pl.ds(0, (rows - 1) * SIDE)
    remote(
        scal_ref.at[most], scal_ref.at[most], scal_sem.at[2], scal_sem.at[3], seq_at(me)
    ).wait_recv()
    level = jnp.full((1, 128), NEG, F32)
    for s in range(shards):
        pair = scal_ref[s]
        stab_s, thr_s = pair[0:1, :], pair[1:2, :]
        m_rows[s : s + 1, :] = level
        carried_on = level + thr_s
        level = jnp.maximum(stab_s, carried_on)
        stab_rows[s : s + 1, :] = stab_s - level
        thr_rows[s : s + 1, :] = carried_on - level
    a_rows[...] = jnp.exp(thr_rows[...])
    b_rows[...] = jnp.exp(stab_rows[...])

    most_tiles = pl.ds(0, shards - 1)
    remote(
        got_tiles.at[most_tiles],
        got_tiles.at[most_tiles],
        tile_sem.at[0],
        tile_sem.at[1],
        seq_at(me),
    ).wait_recv()
    some_norm = pl.ds(0, SIDE - 1)
    remote(
        norm_z.at[some_norm], norm_z.at[some_norm], norm_sem.at[0], norm_sem.at[1], seq_at(me)
    ).wait_recv()
    total = jnp.zeros((2, 128), F32)
    for z in range(SIDE):
        at = pl.ds(my_y * SIDE + z, 1)
        total = a_rows[at, :] * total + b_rows[at, :] * norm_z[z]
    norm_y[my_y] = total
    for step in range(1, rows):
        remote(
            norm_y.at[my_y], norm_y.at[my_y], norm_sem.at[2], norm_sem.at[3], seq_at(y_peer(step))
        ).start()

    state = jnp.zeros((16, 128), F32)
    for s in range(shards):
        back_tiles[s] = state.astype(BF16)
        state = a_rows[s : s + 1, :] * state + b_rows[s : s + 1, :] * got_tiles[s].astype(F32)

    def send_back(peer):
        remote(
            back_tiles.at[peer], mem_tiles.at[me], tile_sem.at[2], tile_sem.at[3], seq_at(peer)
        ).start()

    def to_first(step):
        peer = ((my_y + step) % rows) * SIDE
        pl.when((peer != 0) & (peer != me))(functools.partial(send_back, peer))

    def to_other(step):
        peer = peer_at(step)
        pl.when(peer % SIDE != 0)(functools.partial(send_back, peer))

    for step in (4, 3, 5, 2, 6, 1, 7, 0):
        to_first(step)
    for step in steps:
        to_other(step)

    @pl.when(me == 0)
    def _():
        mem_tiles[...] = jnp.zeros(mem_tiles.shape, BF16)

    @pl.when(me != 0)
    def _():
        mem_tiles[me] = back_tiles[me]


    m_in = m_rows[pl.ds(me, 1), :][:, 0:1]
    begin_full = jnp.concatenate([begin_col] * (tokens // 128), axis=1)
    allowed = (s_full <= t_full) & (s_full >= begin_full)
    log_weight = jnp.where(allowed, gain_row + cum_col, NEG)
    carried = jnp.where(begin_col[:, 0:1] < 0, m_in + cum_col, NEG)
    row_max = jnp.maximum(jnp.max(log_weight, axis=1, keepdims=True), carried)
    weights = scores * jnp.exp(log_weight - row_max)
    reach = jnp.exp(carried - row_max) * scale
    num_ref[...] = jnp.dot(weights.astype(BF16), value, preferred_element_type=F32)
    den_inside = jnp.sum(weights, axis=1, keepdims=True)


    some_y = pl.ds(0, rows - 1)
    remote(
        norm_y.at[some_y], norm_y.at[some_y], norm_sem.at[2], norm_sem.at[3], seq_at(me)
    ).wait_recv()
    norm_in = jnp.zeros((2, 128), F32)
    for y in range(rows):
        decay = a_rows[y * SIDE : y * SIDE + 1, :]
        for z in range(1, SIDE):
            decay = decay * a_rows[y * SIDE + z : y * SIDE + z + 1, :]
        norm_in = jnp.where(y < my_y, decay * norm_in + norm_y[y], norm_in)
    for z in range(SIDE):
        at = pl.ds(my_y * SIDE + z, 1)
        norm_in = jnp.where(
            z < my_z, a_rows[at, :] * norm_in + b_rows[at, :] * norm_z[z], norm_in
        )
    norm_row = jnp.concatenate([norm_in[0:1, :], norm_in[1:2, :]], axis=1)
    from_normal = jnp.sum(query.astype(F32) * norm_row, axis=1, keepdims=True)
    floor = jnp.maximum(jnp.abs(den_inside + reach * from_normal), 1.0)
    inverse = 1.0 / floor

    loads[6].wait()
    @pl.when(me != 0)
    def _():
        remote(
            mem_tiles.at[most_tiles],
            mem_tiles.at[most_tiles],
            tile_sem.at[2],
            tile_sem.at[3],
            seq_at(me),
        ).wait_recv()

    parts = []
    for c in range(values // 128):
        block = mem_tiles[c * tile_rows : (c + 1) * tile_rows].reshape(width, 128)
        from_memory = jnp.dot(query, block, preferred_element_type=F32)
        at = slice(c * 128, (c + 1) * 128)
        parts.append(((num_ref[:, at] + reach * from_memory) * inverse).astype(BF16))
    head_out = jnp.concatenate(parts, axis=1)

    out_cols = out_ref.shape[1]
    half = tokens // 2

    def project(x, core):
        column = pl.multiple_of((2 * x + core) * out_cols, out_cols)
        return jnp.dot(head_out, wo_ref[:, pl.ds(column, out_cols)], preferred_element_type=F32)

    pair_copies = {}

    def pair_start(step):
        pair_send[step] = project((my_x + step) % chips, 1 - my_c).astype(BF16)
        pair_copies[step] = remote(
            pair_send.at[step],
            pair_recv.at[step],
            pair_ssem.at[step],
            pair_rsem.at[step],
            head_at(partner),
        )
        pair_copies[step].start()

    def chip_sum(step):
        ours = project((my_x + step) % chips, my_c)
        pair_copies[step].wait_recv()
        return ours + pair_recv[step].astype(F32)

    quarter = half // 2

    def x_copy(index, slot, count, where):
        slots = pl.ds(slot, count)
        return remote(
            x_send.at[slots], x_recv.at[slots], x_ssem.at[index], x_rsem.at[index], head_at(where)
        )

    x_copies = [
        x_copy(index, slot, count, where)
        for index, (slot, count, where) in enumerate(
            (
                (0, 1, x_next),
                (1, 1, x_next),
                (2, 1, x_prev),
                (3, 1, x_prev),
                (4, 2, x_next),
                (6, 2, x_prev),
                (8, 1, x_next),
                (9, 1, x_next),
                (10, 1, x_prev),
                (11, 1, x_prev),
            )
        )
    ]

    def rows_of(block, index):
        return block[index * quarter : (index + 1) * quarter]

    pair_start(2)
    pair_start(1)
    pair_start(3)
    pair_start(0)
    opposite = chip_sum(2)
    for index in (0, 2, 1, 3):
        x_send[index] = rows_of(opposite, index).astype(BF16)
        x_copies[index].start()
    after = chip_sum(1)
    for index in (2, 3):
        x_send[2 + index] = rows_of(after, index).astype(BF16)
    x_copies[4].start()
    before = chip_sum(3)
    for index in (0, 1):
        x_send[6 + index] = rows_of(before, index).astype(BF16)
    x_copies[5].start()
    for index in (0, 2, 1, 3):
        x_copies[index].wait_recv()
        block = after if index < 2 else before
        x_send[8 + index] = (rows_of(block, index) + x_recv[index].astype(F32)).astype(BF16)
        x_copies[6 + index].start()
    both = chip_sum(0)
    x_copies[4].wait_recv()
    x_copies[5].wait_recv()
    for index in (0, 2, 1, 3):
        straight = x_recv[6 + index] if index < 2 else x_recv[2 + index]
        part = rows_of(both, index) + straight.astype(F32)
        x_copies[6 + index].wait_recv()
        out_ref[index * quarter : (index + 1) * quarter] = (
            part + x_recv[8 + index].astype(F32)
        ).astype(BF16)

    for copy in halos:
        copy.wait_send()
    remote(
        scal_ref.at[some], scal_ref.at[some], scal_sem.at[0], scal_sem.at[1], seq_at(me)
    ).wait_send()
    remote(
        scal_ref.at[most], scal_ref.at[most], scal_sem.at[2], scal_sem.at[3], seq_at(me)
    ).wait_send()
    remote(
        norm_z.at[some_norm], norm_z.at[some_norm], norm_sem.at[0], norm_sem.at[1], seq_at(me)
    ).wait_send()
    remote(
        norm_y.at[some_y], norm_y.at[some_y], norm_sem.at[2], norm_sem.at[3], seq_at(me)
    ).wait_send()
    remote(
        own_tiles.at[most_tiles], own_tiles.at[most_tiles], tile_sem.at[0], tile_sem.at[1], seq_at(me)
    ).wait_send()
    back_sent = pl.ds(0, shards - 2)
    remote(
        back_tiles.at[back_sent], back_tiles.at[back_sent], tile_sem.at[2], tile_sem.at[3], seq_at(me)
    ).wait_send()

    @pl.when(me == 0)
    def _():
        remote(
            back_tiles.at[0], back_tiles.at[0], tile_sem.at[2], tile_sem.at[3], seq_at(me)
        ).wait_send()

    for copy in list(pair_copies.values()) + x_copies:
        copy.wait_send()


def on_device(
    shards,
    chips,
    query_input,
    key_input,
    value_input,
    kernel_taps,
    input_gate,
    forget_gate,
    request_lengths,
    output_weight,
):
    tokens, width = query_input.shape
    values = value_input.shape[1]
    out_cols = output_weight.shape[1] // (2 * chips)
    vmem = pl.BlockSpec(memory_space=pltpu.VMEM)
    dma = pltpu.SemaphoreType.DMA
    return pl.pallas_call(
        functools.partial(kernel, shards, chips),
        out_shape=jax.ShapeDtypeStruct((tokens, out_cols), BF16),
        in_specs=[pl.BlockSpec(memory_space=pltpu.HBM)] * 8,
        out_specs=vmem,
        scratch_shapes=[pltpu.SMEM(request_lengths.shape, jnp.int32)]
        + [
            pltpu.VMEM(a.shape, a.dtype)
            for a in (
                query_input,
                key_input,
                value_input,
                kernel_taps,
                input_gate,
                forget_gate,
            )
        ]
        + [
            pltpu.VMEM(output_weight.shape, BF16),
            pltpu.VMEM((tokens + 8, width), F32),
            pltpu.VMEM((2, 16, width), BF16),
            pltpu.VMEM((shards, 2, 128), F32),
            pltpu.VMEM((shards, 128), F32),
            pltpu.VMEM((shards, 128), F32),
            pltpu.VMEM((shards, 128), F32),
            pltpu.VMEM((shards, 128), F32),
            pltpu.VMEM((shards, 128), F32),
            pltpu.VMEM((shards, 16, 128), BF16),
            pltpu.VMEM((shards, 16, 128), BF16),
            pltpu.VMEM((shards, 16, 128), BF16),
            pltpu.VMEM((shards, 16, 128), BF16),
            pltpu.VMEM((SIDE, 2, 128), F32),
            pltpu.VMEM((shards // SIDE, 2, 128), F32),
            pltpu.VMEM((tokens, values), F32),
            pltpu.VMEM((chips, tokens, out_cols), BF16),
            pltpu.VMEM((chips, tokens, out_cols), BF16),
            pltpu.VMEM((12, tokens // 4, out_cols), BF16),
            pltpu.VMEM((12, tokens // 4, out_cols), BF16),
            dma((8,)),
            dma((4,)),
            dma((4,)),
            dma((4,)),
            dma((4,)),
            dma((chips,)),
            dma((chips,)),
            dma((10,)),
            dma((10,)),
            pltpu.SemaphoreType.REGULAR,
        ],
        compiler_params=pltpu.CompilerParams(
            collective_id=0, has_side_effects=True, vmem_limit_bytes=32 << 20
        ),
    )(
        *(
            pltpu.with_memory_space_constraint(a, pltpu.HBM)
            for a in (
                request_lengths,
                query_input,
                key_input,
                value_input,
                kernel_taps,
                input_gate,
                forget_gate,
                output_weight,
            )
        ),
    )


def solution(mesh):
    placed = (
        P("seq", "head"),
        P("seq", "head"),
        P("seq", "head"),
        P(None, None, "head"),
        P("head", "seq"),
        P("head", "seq"),
        P(),
        P("head", None),
    )
    return jax.shard_map(
        functools.partial(on_device, mesh.shape["seq"], mesh.shape["head"] // 2),
        mesh=mesh,
        in_specs=placed,
        out_specs=P("seq", "head"),
        check_vma=False,
    )
```

```python
import functools

import jax
import jax.numpy as jnp
from jax import lax
from jax.experimental import pallas as pl
from jax.experimental.pallas import tpu as pltpu
from jax.sharding import PartitionSpec as P

MESH = pl.DeviceIdType.MESH
NEG = -1e30
SIDE = 8
F32 = jnp.float32
BF16 = jnp.bfloat16


def kernel(
    shards,
    chips,
    len_hbm,
    q_hbm,
    k_hbm,
    v_hbm,
    taps_hbm,
    ig_hbm,
    fg_hbm,
    wo_hbm,
    out_ref,
    len_ref,
    q_ref,
    k_ref,
    v_ref,
    taps_ref,
    ig_ref,
    fg_ref,
    wo_ref,
    ext_ref,
    halo_recv,
    scal_ref,
    stab_rows,
    thr_rows,
    m_rows,
    a_rows,
    b_rows,
    own_tiles,
    got_tiles,
    back_tiles,
    mem_tiles,
    norm_z,
    norm_y,
    num_ref,
    pair_send,
    pair_recv,
    x_send,
    x_recv,
    load_sem,
    halo_sem,
    scal_sem,
    norm_sem,
    tile_sem,
    pair_ssem,
    pair_rsem,
    x_ssem,
    x_rsem,
    rows_sem,
):
    tokens, width = q_hbm.shape
    values = v_hbm.shape[1]
    scale = 1.0 / (width**0.5)
    me = lax.axis_index("seq")
    head = lax.axis_index("head")
    my_y, my_z = me // SIDE, me % SIDE
    my_x, my_c = head // 2, head % 2
    rows = shards // SIDE

    def seq_at(index):
        return {"seq": index}

    def head_at(index):
        return {"head": index}

    def remote(src, dst, ssem, rsem, where):
        return pltpu.make_async_remote_copy(
            src_ref=src, dst_ref=dst, send_sem=ssem, recv_sem=rsem, device_id=where, device_id_type=MESH
        )

    barrier = pltpu.get_barrier_semaphore()

    def z_peer(step):
        return my_y * SIDE + (my_z + step) % SIDE

    def y_peer(step):
        return ((my_y + step) % rows) * SIDE + my_z

    partner = 2 * my_x + (1 - my_c)
    x_next = 2 * ((my_x + 1) % chips) + my_c
    x_prev = 2 * ((my_x + chips - 1) % chips) + my_c
    known = [seq_at((me + shards - 1) % shards)]
    known += [seq_at(z_peer(step)) for step in (4, 3, 5, 2, 6, 1, 7)]
    known += [seq_at(y_peer(step)) for step in (4, 3, 5, 2, 6, 1, 7)]
    known += [head_at(partner), head_at(x_next), head_at(x_prev)]
    for where in known:
        pl.semaphore_signal(barrier, inc=1, device_id=where, device_id_type=MESH)

    loads = [
        pltpu.make_async_copy(src, dst, load_sem.at[i])
        for i, (src, dst) in enumerate(
            (
                (fg_hbm, fg_ref),
                (ig_hbm, ig_ref),
                (k_hbm, k_ref),
                (q_hbm, q_ref),
                (taps_hbm, taps_ref),
                (v_hbm, v_ref),
                (wo_hbm, wo_ref),
                (len_hbm, len_ref),
            )
        )
    ]
    for load in loads:
        load.start()

    loads[7].wait()
    offset = me * tokens
    starts = [jnp.int32(0)]
    for r in range(len_ref.shape[0] - 1):
        starts.append(starts[-1] + len_ref[r])

    def request_start(position):
        found = jnp.zeros_like(position)
        for start in starts[1:]:
            found = jnp.where(start <= position, start, found)
        return found

    t_col = lax.broadcasted_iota(jnp.int32, (tokens, 128), 0)
    begin_col = request_start(t_col + offset) - offset
    s_row = lax.broadcasted_iota(jnp.int32, (1, tokens), 1)
    last_begin = jnp.int32(0)
    for start in starts[1:]:
        last_begin = jnp.where(start <= offset + (tokens - 1), start, last_begin)
    last_begin = last_begin - offset

    loads[0].wait()
    loads[1].wait()
    fg = fg_ref[...]
    ig = ig_ref[...]
    log_forget = -(jnp.maximum(-fg, 0.0) + jnp.log1p(jnp.exp(-jnp.abs(fg))))
    hi = log_forget.astype(BF16)
    rest = log_forget - hi.astype(F32)
    mid = rest.astype(BF16)
    low = (rest - mid.astype(F32)).astype(BF16)
    pieces = jnp.concatenate(
        [hi.astype(F32), mid.astype(F32), low.astype(F32), jnp.zeros((5, tokens), F32)], axis=0
    ).astype(BF16)
    t_full = lax.broadcasted_iota(jnp.int32, (tokens, tokens), 0)
    s_full = lax.broadcasted_iota(jnp.int32, (tokens, tokens), 1)
    upper = jnp.where(t_full <= s_full, 1.0, 0.0).astype(BF16)
    cum_row = jnp.sum(
        jnp.dot(pieces, upper, preferred_element_type=F32), axis=0, keepdims=True
    )
    cum_last = cum_row[:, tokens - 1 : tokens]
    gain_row = ig - cum_row
    tail_row = jnp.where(s_row >= last_begin, gain_row + cum_last, NEG)
    stab = jnp.max(tail_row, axis=1, keepdims=True)
    factor_row = jnp.exp(tail_row - stab)
    through = jnp.where(last_begin < 0, cum_last, NEG)
    scal_ref[me] = jnp.concatenate(
        [jnp.broadcast_to(stab, (1, 128)), jnp.broadcast_to(through, (1, 128))], axis=0
    )
    turned = jnp.transpose(
        jnp.concatenate([cum_row, factor_row, jnp.zeros((126, tokens), F32)], axis=0)
    )
    cum_col = turned[:, 0:1]
    factor_col = turned[:, 1:2]

    loads[2].wait()
    loads[3].wait()
    pl.semaphore_wait(barrier, len(known))

    tail = pl.ds(tokens - 16, 16)
    follower = seq_at((me + 1) % shards)
    halos = [
        remote(ref.at[tail, :], halo_recv.at[i], halo_sem.at[2 * i], halo_sem.at[2 * i + 1], follower)
        for i, ref in enumerate((k_ref, q_ref))
    ]
    halos[0].start()
    for step in (4, 3, 5, 2, 6, 1, 7):
        pl.semaphore_signal(
            rows_sem, inc=1, device_id=seq_at(y_peer(step)), device_id_type=MESH
        )
    for step in (4, 3, 5, 2, 6, 1, 7):
        remote(
            scal_ref.at[me], scal_ref.at[me], scal_sem.at[0], scal_sem.at[1], seq_at(z_peer(step))
        ).start()
    halos[1].start()

    def conv_silu(which, first, count):
        begin = begin_col[first : first + count]
        position = t_col[first : first + count]
        running = taps_ref[which, 0:1, :] * ext_ref[8 + first : 8 + first + count, :]
        for lag in range(1, taps_ref.shape[1]):
            keep = (position - lag) >= begin
            keep = jnp.concatenate([keep.astype(F32)] * (width // 128), axis=1) > 0.0
            shifted = ext_ref[8 + first - lag : 8 + first - lag + count, :]
            running = running + jnp.where(keep, taps_ref[which, lag : lag + 1, :] * shifted, 0.0)
        return (running / (1.0 + jnp.exp(-running))).astype(BF16)

    def outer_sum(left, right):
        return lax.dot_general(
            left, right, (((0,), (0,)), ((), ())), preferred_element_type=F32
        )

    loads[4].wait()
    loads[5].wait()
    ext_ref[8 : 8 + tokens, :] = k_ref[...].astype(F32)
    key_rest = conv_silu(1, 16, tokens - 16)
    weighted_rest = key_rest.astype(F32) * factor_col[16:]
    memory_rest = outer_sum(weighted_rest.astype(BF16), v_ref[16:, :])
    normal_rest = jnp.sum(weighted_rest, axis=0, keepdims=True)
    halos[0].wait_recv()
    ext_ref[0:8, :] = halo_recv[0, 8:16, :].astype(F32)
    key_first = conv_silu(1, 0, 16)
    weighted_first = key_first.astype(F32) * factor_col[:16]
    memory = (memory_rest + outer_sum(weighted_first.astype(BF16), v_ref[:16, :])).astype(BF16)
    key = jnp.concatenate([key_first, key_rest], axis=0)
    value = v_ref[...]
    tile_rows = width // 16
    for c in range(values // 128):
        own_tiles[c * tile_rows : (c + 1) * tile_rows] = memory[
            :, c * 128 : (c + 1) * 128
        ].reshape(tile_rows, 16, 128)
    normal = normal_rest + jnp.sum(weighted_first, axis=0, keepdims=True)
    norm_z[my_z] = jnp.concatenate([normal[:, 0:128], normal[:, 128:256]], axis=0)

    def far(step):
        dy, dz = step // SIDE, step % SIDE
        return -(min(dy, rows - dy) + min(dz, SIDE - dz))

    steps = sorted(range(1, shards), key=far)

    def peer_at(step):
        return ((my_y + step // SIDE) % rows) * SIDE + (my_z + step % SIDE) % SIDE

    def send_tiles(chosen):
        for step in chosen:
            peer = peer_at(step)
            remote(
                own_tiles.at[peer], got_tiles.at[me], tile_sem.at[0], tile_sem.at[1], seq_at(peer)
            ).start()

    pl.semaphore_wait(rows_sem, rows - 1)
    send_tiles(steps[:24])

    some = pl.ds(0, SIDE - 1)
    remote(
        scal_ref.at[some], scal_ref.at[some], scal_sem.at[0], scal_sem.at[1], seq_at(me)
    ).wait_recv()
    mine = pl.ds(my_y * SIDE, SIDE)
    for step in range(1, rows):
        remote(
            scal_ref.at[mine],
            scal_ref.at[mine],
            scal_sem.at[2],
            scal_sem.at[3],
            seq_at(y_peer(step)),
        ).start()
    send_tiles(steps[24:])
    for step in range(1, SIDE):
        remote(
            norm_z.at[my_z], norm_z.at[my_z], norm_sem.at[0], norm_sem.at[1], seq_at(z_peer(step))
        ).start()
    got_tiles[me] = own_tiles[me]

    halos[1].wait_recv()
    ext_ref[0:8, :] = halo_recv[1, 8:16, :].astype(F32)
    ext_ref[8 : 8 + tokens, :] = q_ref[...].astype(F32)
    query = conv_silu(0, 0, tokens)
    scores = (
        lax.dot_general(query, key, (((1,), (1,)), ((), ())), preferred_element_type=F32) * scale
    )

    most = pl.ds(0, (rows - 1) * SIDE)
    remote(
        scal_ref.at[most], scal_ref.at[most], scal_sem.at[2], scal_sem.at[3], seq_at(me)
    ).wait_recv()
    level = jnp.full((1, 128), NEG, F32)
    for s in range(shards):
        pair = scal_ref[s]
        stab_s, thr_s = pair[0:1, :], pair[1:2, :]
        m_rows[s : s + 1, :] = level
        carried_on = level + thr_s
        level = jnp.maximum(stab_s, carried_on)
        stab_rows[s : s + 1, :] = stab_s - level
        thr_rows[s : s + 1, :] = carried_on - level
    a_rows[...] = jnp.exp(thr_rows[...])
    b_rows[...] = jnp.exp(stab_rows[...])

    most_tiles = pl.ds(0, shards - 1)
    remote(
        got_tiles.at[most_tiles],
        got_tiles.at[most_tiles],
        tile_sem.at[0],
        tile_sem.at[1],
        seq_at(me),
    ).wait_recv()
    some_norm = pl.ds(0, SIDE - 1)
    remote(
        norm_z.at[some_norm], norm_z.at[some_norm], norm_sem.at[0], norm_sem.at[1], seq_at(me)
    ).wait_recv()
    total = jnp.zeros((2, 128), F32)
    for z in range(SIDE):
        at = pl.ds(my_y * SIDE + z, 1)
        total = a_rows[at, :] * total + b_rows[at, :] * norm_z[z]
    norm_y[my_y] = total
    for step in range(1, rows):
        remote(
            norm_y.at[my_y], norm_y.at[my_y], norm_sem.at[2], norm_sem.at[3], seq_at(y_peer(step))
        ).start()

    state = jnp.zeros((16, 128), F32)
    for s in range(shards):
        back_tiles[s] = state.astype(BF16)
        state = a_rows[s : s + 1, :] * state + b_rows[s : s + 1, :] * got_tiles[s].astype(F32)

    my_half = my_y // (rows // 2)

    def send_back(peer):
        remote(
            back_tiles.at[peer],
            mem_tiles.at[me],
            tile_sem.at[2],
            tile_sem.at[3 + my_half],
            seq_at(peer),
        ).start()

    def to_first(step):
        peer = ((my_y + step) % rows) * SIDE
        pl.when((peer != 0) & (peer != me))(functools.partial(send_back, peer))

    def to_other(step):
        peer = peer_at(step)
        pl.when(peer % SIDE != 0)(functools.partial(send_back, peer))

    for step in (4, 3, 5, 2, 6, 1, 7, 0):
        to_first(step)
    for step in steps:
        to_other(step)

    @pl.when(me == 0)
    def _():
        mem_tiles[...] = jnp.zeros(mem_tiles.shape, BF16)

    @pl.when(me != 0)
    def _():
        pltpu.make_async_copy(
            back_tiles.at[me], mem_tiles.at[me], tile_sem.at[3 + my_half]
        ).start()


    m_in = m_rows[pl.ds(me, 1), :][:, 0:1]
    begin_full = jnp.concatenate([begin_col] * (tokens // 128), axis=1)
    allowed = (s_full <= t_full) & (s_full >= begin_full)
    log_weight = jnp.where(allowed, gain_row + cum_col, NEG)
    carried = jnp.where(begin_col[:, 0:1] < 0, m_in + cum_col, NEG)
    row_max = jnp.maximum(jnp.max(log_weight, axis=1, keepdims=True), carried)
    weights = scores * jnp.exp(log_weight - row_max)
    reach = jnp.exp(carried - row_max) * scale
    num_ref[...] = jnp.dot(weights.astype(BF16), value, preferred_element_type=F32)
    den_inside = jnp.sum(weights, axis=1, keepdims=True)


    some_y = pl.ds(0, rows - 1)
    remote(
        norm_y.at[some_y], norm_y.at[some_y], norm_sem.at[2], norm_sem.at[3], seq_at(me)
    ).wait_recv()
    norm_in = jnp.zeros((2, 128), F32)
    for y in range(rows):
        decay = a_rows[y * SIDE : y * SIDE + 1, :]
        for z in range(1, SIDE):
            decay = decay * a_rows[y * SIDE + z : y * SIDE + z + 1, :]
        norm_in = jnp.where(y < my_y, decay * norm_in + norm_y[y], norm_in)
    for z in range(SIDE):
        at = pl.ds(my_y * SIDE + z, 1)
        norm_in = jnp.where(
            z < my_z, a_rows[at, :] * norm_in + b_rows[at, :] * norm_z[z], norm_in
        )
    norm_row = jnp.concatenate([norm_in[0:1, :], norm_in[1:2, :]], axis=1)
    from_normal = jnp.sum(query.astype(F32) * norm_row, axis=1, keepdims=True)
    floor = jnp.maximum(jnp.abs(den_inside + reach * from_normal), 1.0)
    inverse = 1.0 / floor

    loads[6].wait()
    def head_half(which):
        tiles = pl.ds(which * shards // 2, shards // 2)

        @pl.when(me != 0)
        def _():
            remote(
                mem_tiles.at[tiles],
                mem_tiles.at[tiles],
                tile_sem.at[2],
                tile_sem.at[3 + which],
                seq_at(me),
            ).wait_recv()

        parts = []
        for c in range(which * values // 256, (which + 1) * values // 256):
            block = mem_tiles[c * tile_rows : (c + 1) * tile_rows].reshape(width, 128)
            from_memory = jnp.dot(query, block, preferred_element_type=F32)
            at = slice(c * 128, (c + 1) * 128)
            parts.append(((num_ref[:, at] + reach * from_memory) * inverse).astype(BF16))
        return jnp.concatenate(parts, axis=1)

    head_out = jnp.concatenate([head_half(0), head_half(1)], axis=1)

    out_cols = out_ref.shape[1]
    half = tokens // 2

    def project(x, core):
        column = pl.multiple_of((2 * x + core) * out_cols, out_cols)
        return jnp.dot(head_out, wo_ref[:, pl.ds(column, out_cols)], preferred_element_type=F32)

    pair_copies = {}

    def pair_start(step):
        pair_send[step] = project((my_x + step) % chips, 1 - my_c).astype(BF16)
        pair_copies[step] = remote(
            pair_send.at[step],
            pair_recv.at[step],
            pair_ssem.at[step],
            pair_rsem.at[step],
            head_at(partner),
        )
        pair_copies[step].start()

    def chip_sum(step):
        ours = project((my_x + step) % chips, my_c)
        pair_copies[step].wait_recv()
        return ours + pair_recv[step].astype(F32)

    quarter = half // 2

    def x_copy(index, slot, count, where):
        slots = pl.ds(slot, count)
        return remote(
            x_send.at[slots], x_recv.at[slots], x_ssem.at[index], x_rsem.at[index], head_at(where)
        )

    x_copies = [
        x_copy(index, slot, count, where)
        for index, (slot, count, where) in enumerate(
            (
                (0, 1, x_next),
                (1, 1, x_next),
                (2, 1, x_prev),
                (3, 1, x_prev),
                (4, 2, x_next),
                (6, 2, x_prev),
                (8, 1, x_next),
                (9, 1, x_next),
                (10, 1, x_prev),
                (11, 1, x_prev),
            )
        )
    ]

    def rows_of(block, index):
        return block[index * quarter : (index + 1) * quarter]

    pair_start(2)
    pair_start(1)
    pair_start(3)
    pair_start(0)
    opposite = chip_sum(2)
    for index in (0, 2, 1, 3):
        x_send[index] = rows_of(opposite, index).astype(BF16)
        x_copies[index].start()
    after = chip_sum(1)
    for index in (2, 3):
        x_send[2 + index] = rows_of(after, index).astype(BF16)
    x_copies[4].start()
    before = chip_sum(3)
    for index in (0, 1):
        x_send[6 + index] = rows_of(before, index).astype(BF16)
    x_copies[5].start()
    for index in (0, 2, 1, 3):
        x_copies[index].wait_recv()
        block = after if index < 2 else before
        x_send[8 + index] = (rows_of(block, index) + x_recv[index].astype(F32)).astype(BF16)
        x_copies[6 + index].start()
    both = chip_sum(0)
    x_copies[4].wait_recv()
    x_copies[5].wait_recv()
    for index in (0, 2, 1, 3):
        straight = x_recv[6 + index] if index < 2 else x_recv[2 + index]
        part = rows_of(both, index) + straight.astype(F32)
        x_copies[6 + index].wait_recv()
        out_ref[index * quarter : (index + 1) * quarter] = (
            part + x_recv[8 + index].astype(F32)
        ).astype(BF16)

    for copy in halos:
        copy.wait_send()
    remote(
        scal_ref.at[some], scal_ref.at[some], scal_sem.at[0], scal_sem.at[1], seq_at(me)
    ).wait_send()
    remote(
        scal_ref.at[most], scal_ref.at[most], scal_sem.at[2], scal_sem.at[3], seq_at(me)
    ).wait_send()
    remote(
        norm_z.at[some_norm], norm_z.at[some_norm], norm_sem.at[0], norm_sem.at[1], seq_at(me)
    ).wait_send()
    remote(
        norm_y.at[some_y], norm_y.at[some_y], norm_sem.at[2], norm_sem.at[3], seq_at(me)
    ).wait_send()
    remote(
        own_tiles.at[most_tiles], own_tiles.at[most_tiles], tile_sem.at[0], tile_sem.at[1], seq_at(me)
    ).wait_send()
    back_sent = pl.ds(0, shards - 2)
    remote(
        back_tiles.at[back_sent], back_tiles.at[back_sent], tile_sem.at[2], tile_sem.at[3], seq_at(me)
    ).wait_send()

    @pl.when(me == 0)
    def _():
        remote(
            back_tiles.at[0], back_tiles.at[0], tile_sem.at[2], tile_sem.at[3], seq_at(me)
        ).wait_send()

    for copy in list(pair_copies.values()) + x_copies:
        copy.wait_send()


def on_device(
    shards,
    chips,
    query_input,
    key_input,
    value_input,
    kernel_taps,
    input_gate,
    forget_gate,
    request_lengths,
    output_weight,
):
    tokens, width = query_input.shape
    values = value_input.shape[1]
    out_cols = output_weight.shape[1] // (2 * chips)
    vmem = pl.BlockSpec(memory_space=pltpu.VMEM)
    dma = pltpu.SemaphoreType.DMA
    return pl.pallas_call(
        functools.partial(kernel, shards, chips),
        out_shape=jax.ShapeDtypeStruct((tokens, out_cols), BF16),
        in_specs=[pl.BlockSpec(memory_space=pltpu.HBM)] * 8,
        out_specs=vmem,
        scratch_shapes=[pltpu.SMEM(request_lengths.shape, jnp.int32)]
        + [
            pltpu.VMEM(a.shape, a.dtype)
            for a in (
                query_input,
                key_input,
                value_input,
                kernel_taps,
                input_gate,
                forget_gate,
            )
        ]
        + [
            pltpu.VMEM(output_weight.shape, BF16),
            pltpu.VMEM((tokens + 8, width), F32),
            pltpu.VMEM((2, 16, width), BF16),
            pltpu.VMEM((shards, 2, 128), F32),
            pltpu.VMEM((shards, 128), F32),
            pltpu.VMEM((shards, 128), F32),
            pltpu.VMEM((shards, 128), F32),
            pltpu.VMEM((shards, 128), F32),
            pltpu.VMEM((shards, 128), F32),
            pltpu.VMEM((shards, 16, 128), BF16),
            pltpu.VMEM((shards, 16, 128), BF16),
            pltpu.VMEM((shards, 16, 128), BF16),
            pltpu.VMEM((shards, 16, 128), BF16),
            pltpu.VMEM((SIDE, 2, 128), F32),
            pltpu.VMEM((shards // SIDE, 2, 128), F32),
            pltpu.VMEM((tokens, values), F32),
            pltpu.VMEM((chips, tokens, out_cols), BF16),
            pltpu.VMEM((chips, tokens, out_cols), BF16),
            pltpu.VMEM((12, tokens // 4, out_cols), BF16),
            pltpu.VMEM((12, tokens // 4, out_cols), BF16),
            dma((8,)),
            dma((4,)),
            dma((4,)),
            dma((4,)),
            dma((5,)),
            dma((chips,)),
            dma((chips,)),
            dma((10,)),
            dma((10,)),
            pltpu.SemaphoreType.REGULAR,
        ],
        compiler_params=pltpu.CompilerParams(
            collective_id=0, has_side_effects=True, vmem_limit_bytes=32 << 20
        ),
    )(
        *(
            pltpu.with_memory_space_constraint(a, pltpu.HBM)
            for a in (
                request_lengths,
                query_input,
                key_input,
                value_input,
                kernel_taps,
                input_gate,
                forget_gate,
                output_weight,
            )
        ),
    )


def solution(mesh):
    placed = (
        P("seq", "head"),
        P("seq", "head"),
        P("seq", "head"),
        P(None, None, "head"),
        P("head", "seq"),
        P("head", "seq"),
        P(),
        P("head", None),
    )
    return jax.shard_map(
        functools.partial(on_device, mesh.shape["seq"], mesh.shape["head"] // 2),
        mesh=mesh,
        in_specs=placed,
        out_specs=P("seq", "head"),
        check_vma=False,
    )
```
